256 devices in a mesh: expert: 4 (over z_lo), etp: 16 (over y, x), tp: 4 (over z_hi, core).
Axes of the slice: x: 4, y: 4, z: 8 (z_hi: 2, z_lo: 4; z = z_hi * 4 + z_lo), core: 2. Of those that a mesh axis runs over, the one named last changes fastest.
Arguments:
- d_out: bfloat16 [2048, 6144], P(('expert', 'tp'), 'etp'), may hold values from -6 to 6
- expert_ids: int32 [2048, 2], P(('expert', 'tp')), may hold values from 0 to 3, all different within a row; in each aligned block of 128 rows (0 to 127, 128 to 255, ...) at most 64 rows name the same one
- gate_weights: float32 [2048, 2], P(('expert', 'tp')), may hold values from 0.05 to 0.95, as said below
- saved_gate: bfloat16 [4, 1024, 16384], P('expert', None, ('etp', 'tp')), may hold values from -8 to 8
- saved_up: bfloat16 [4, 1024, 16384], P('expert', None, ('etp', 'tp')), may hold values from -6 to 6
- w_gate: bfloat16 [4, 6144, 16384], P('expert', None, ('etp', 'tp')), may hold values from -0.078125 to 0.078125
- w_up: bfloat16 [4, 6144, 16384], P('expert', None, ('etp', 'tp')), may hold values from -0.078125 to 0.078125
- w_down: bfloat16 [4, 16384, 6144], P('expert', ('etp', 'tp')), may hold values from -0.046875 to 0.046875
- w_out: bfloat16 [6144, 6144], P('tp', 'etp'), may hold values from -0.078125 to 0.078125
Outputs:
- d_hidden: bfloat16 [2048, 6144], P(('expert', 'tp'), 'etp')
- d_heads: bfloat16 [2048, 6144], P(('expert', 'etp'), 'tp')
The draws below stay inside these ranges and needn't reach their ends.
Inputs may be any that keep to these rules, and one draw needn't show every extreme that they name: `expert_ids`: each token names two different experts; in every block of 128 tokens every expert is named by exactly 64 tokens. `gate_weights`: a token's two weights sum to one.
All inputs are finite; a program needn't handle non-finite values.
Results may differ from the reference program's by a relative error of at most 0.02.
Values may be sent and summed in bfloat16 or wider, within the bound.
No kernel may reach another device: no remote copies, remote signals or barrier semaphores. Data moves between devices by JAX's collectives and lax.ppermute only.
A program may use at most 128 MiB of HBM per device.

```python
import math
import jax
import jax.numpy as jnp
import numpy as np
from jax import lax

D = 6144
FF = 16384
TOK_GRP = 128
EXPERTS = 4
HD = 6144
CAP = 64
TOKENS = 2048
ROWS = 1024
N_EXPERT = 4
N_ETP = 16
N_TP = 4


def draw_gate_weights(key, part):
    first_weight = jax.random.uniform(key, (TOKENS, 1), jnp.float32, 0.2, 0.8)
    return jnp.concatenate([first_weight, 1.0 - first_weight], axis=1)


def block_levels(own_key, dims, cuts, least, largest):
    gain = 1.0
    for axis_at, shards_of in cuts:
        heights = jax.random.uniform(jax.random.fold_in(jax.random.fold_in(own_key, 6), axis_at), (shards_of,), jnp.float32, least / len(cuts), largest / len(cuts))
        gain = gain * jnp.repeat(jnp.exp(heights), dims[axis_at] // shards_of).reshape((-1,) + (1,) * (len(dims) - 1 - axis_at))
    return gain


def assign_block(rng, own, number, rows, count, top, reach, lean):
    order = jax.random.permutation(rng, count)
    crowded, common = load_shares(count, rows * top, reach, lean, True), load_shares(count, rows * top, reach, lean, False)
    places = jnp.arange(count)

    def named(lengths, rotation):
        used = int((lengths > 0).sum())
        fixed = max(1, used // 4)
        passed = fixed + (places - fixed + rotation * (used - fixed)) % max(1, count - fixed)
        return jnp.zeros((count,), jnp.int32).at[order[jnp.where(places < fixed, places, passed)]].set(jnp.asarray(lengths, jnp.int32))

    lengths = jnp.where(number % 4 == 0, named(crowded, number // 4), named(common, number - number // 4 - 1))
    mixed = jax.random.permutation(jax.random.fold_in(own, 3), count)
    donor, receiver = mixed[0:count // 2 * 2:2], mixed[1:count // 2 * 2:2]
    slack = jnp.minimum(lengths[donor] - 1, reach - lengths[receiver]) // 2
    slack = jnp.where((donor == order[0]) | (receiver == order[0]) | (lengths[receiver] == 0), 0, jnp.maximum(slack, 0))
    passed = jax.random.randint(jax.random.fold_in(own, 4), (count // 2,), 0, 1 << 20) % (slack + 1)
    lengths = lengths.at[donor].add(-passed).at[receiver].add(passed)
    labels = jnp.searchsorted(jnp.cumsum(lengths), jnp.arange(rows * top), side="right").astype(jnp.int32)
    listing = labels.reshape(top, rows).T
    listing = listing[jax.random.permutation(jax.random.fold_in(own, 1), rows)]
    rotation = jax.random.randint(jax.random.fold_in(own, 2), (rows, 1), 0, top)
    return jnp.take_along_axis(listing, (jnp.arange(top)[None, :] + rotation) % top, axis=1)


def load_shares(count, total, bound, slope, full):
    portions = [(1 << 20) // math.isqrt(standing ** slope) + 1 for standing in range(1, count + 1)]
    largest = bound if full else min(bound, max(-(-total // count), total * portions[0] // sum(portions)))
    least = 1 if total - largest >= count - 1 else 0
    counts, spare = [largest] + [least] * (count - 1), total - largest - least * (count - 1)
    while spare > 0:
        candidates = [i for i in range(1, count) if counts[i] < largest] or [i for i in range(1, count) if counts[i] < bound]
        pool, budget = sum([portions[i] for i in candidates]), spare
        for i in candidates:
            extra = min(bound - counts[i], max(1, budget * portions[i] // pool), spare)
            counts[i] = counts[i] + extra
            spare = spare - extra
    return np.array(counts)


def scatter_about(own_key, dims, width, reach, pieces=(), kind=jnp.bfloat16):
    drawn = width * jax.random.normal(own_key, dims, jnp.float32)
    if pieces:
        drawn = drawn * block_levels(own_key, dims, pieces, -0.22, 0.18)
    return jnp.clip(drawn, -reach, reach).astype(kind)


def setup_inputs(seed: int = 0) -> dict:
    key_of = jax.random.split(jax.random.key(seed), 10)
    d_out = scatter_about(key_of[0], (TOKENS, D), 1.0, 6.0, ((0, 16), (1, 16)))
    expert_ids_keys = jax.random.split(jax.random.fold_in(key_of[1], 1), TOKENS // TOK_GRP)
    expert_ids_turns = jax.random.permutation(jax.random.fold_in(key_of[1], 3), TOKENS // TOK_GRP)
    expert_ids = jax.vmap(lambda own, number: assign_block(jax.random.fold_in(key_of[1], 2), own, number, TOK_GRP, EXPERTS, 2, CAP, 0))(expert_ids_keys, expert_ids_turns).reshape((TOKENS, 2))
    gate_weights = draw_gate_weights(jax.random.fold_in(key_of[9], 71), 0)
    saved_gate = scatter_about(key_of[3], (EXPERTS, ROWS, FF), 2.0, 8.0, ((0, 4), (2, 64)))
    saved_up = scatter_about(key_of[4], (EXPERTS, ROWS, FF), 1.0, 6.0, ((0, 4), (2, 64)))
    w_gate = scatter_about(key_of[5], (EXPERTS, D, FF), D ** -0.5, 0.078125, ((0, 4), (2, 64)))
    w_up = scatter_about(key_of[6], (EXPERTS, D, FF), D ** -0.5, 0.078125, ((0, 4), (2, 64)))
    w_down = scatter_about(key_of[7], (EXPERTS, FF, D), FF ** -0.5, 0.046875, ((0, 4), (1, 64)))
    w_out = scatter_about(key_of[8], (HD, D), HD ** -0.5, 0.078125, ((0, 4), (1, 16)))
    return {"d_out": d_out, "expert_ids": expert_ids, "gate_weights": gate_weights, "saved_gate": saved_gate, "saved_up": saved_up, "w_gate": w_gate, "w_up": w_up, "w_down": w_down, "w_out": w_out}


def expert_backward(rows_in, gate_saved, up_saved, gate_matrix, up_matrix, down_matrix):
    grad_act = jnp.dot(rows_in, down_matrix.T, preferred_element_type=jnp.float32)
    gate_val = gate_saved.astype(jnp.float32)
    up_val = up_saved.astype(jnp.float32)
    sigma = jax.nn.sigmoid(gate_val)
    grad_up = (grad_act * gate_val * sigma).astype(jnp.bfloat16)
    grad_gate = (grad_act * up_val * sigma * (1.0 + gate_val * (1.0 - sigma))).astype(jnp.bfloat16)
    run_count = N_ETP * N_TP
    run_len = FF // run_count

    def add_run(index, total):
        start = (index * run_len).astype(jnp.int32)
        gate_piece = lax.dynamic_slice_in_dim(grad_gate, start, run_len, 1)
        up_piece = lax.dynamic_slice_in_dim(grad_up, start, run_len, 1)
        gate_cols = lax.dynamic_slice_in_dim(gate_matrix, start, run_len, 1)
        up_cols = lax.dynamic_slice_in_dim(up_matrix, start, run_len, 1)
        first_part = jnp.dot(gate_piece, gate_cols.T, preferred_element_type=jnp.float32)
        partial_sum = first_part + jnp.dot(up_piece, up_cols.T, preferred_element_type=jnp.float32)
        return total + partial_sum.astype(jnp.bfloat16).astype(jnp.float32)

    initial = jnp.zeros((rows_in.shape[0], gate_matrix.shape[0]), jnp.float32)
    return lax.fori_loop(0, run_count, add_run, initial)


def reference(d_out, expert_ids, gate_weights, saved_gate, saved_up, w_gate, w_up, w_down, w_out):
    owners = N_EXPERT * N_TP
    experts_iota = jnp.arange(EXPERTS, dtype=jnp.int32)
    first_hit = (expert_ids[:, 0:1] == experts_iota[None, :])
    second_hit = (expert_ids[:, 1:2] == experts_iota[None, :])
    member = first_hit.astype(jnp.int32) + second_hit.astype(jnp.int32)
    weight = gate_weights[:, 0:1] * first_hit.astype(jnp.float32) + gate_weights[:, 1:2] * second_hit.astype(jnp.float32)
    member_blk = member.reshape(owners, TOK_GRP, EXPERTS)
    slot = jnp.cumsum(member_blk, axis=1) - member_blk
    slot_iota = jnp.arange(CAP, dtype=jnp.int32)
    select = ((slot[:, :, :, None] == slot_iota[None, None, None, :]) & (member_blk[:, :, :, None] > 0)).astype(jnp.float32)
    weighted_sel = select * weight.reshape(owners, TOK_GRP, EXPERTS)[:, :, :, None]
    grads_blk = d_out.reshape(owners, TOK_GRP, D).astype(jnp.float32)
    dispatched = jnp.einsum("otec,otd->eocd", weighted_sel, grads_blk, precision=lax.Precision.HIGHEST).astype(jnp.bfloat16)
    returned_all = []
    for expert in range(EXPERTS):
        rows_in = dispatched[expert].reshape(owners * CAP, D)
        result = expert_backward(rows_in, saved_gate[expert], saved_up[expert], w_gate[expert], w_up[expert], w_down[expert])
        returned_all.append(result.reshape(owners, CAP, D))
    returned = jnp.stack(returned_all, axis=0)
    d_moe = jnp.einsum("otec,eocd->otd", select, returned, precision=lax.Precision.HIGHEST).reshape(TOKENS, D)
    d_hidden = (d_out.astype(jnp.float32) + d_moe).astype(jnp.bfloat16)
    feat_run = D // N_ETP
    head_total = jnp.zeros((TOKENS, HD), jnp.float32)
    for run in range(N_ETP):
        hidden_piece = d_hidden[:, run * feat_run:(run + 1) * feat_run]
        out_piece = w_out[:, run * feat_run:(run + 1) * feat_run]
        head_piece = jnp.dot(hidden_piece, out_piece.T, preferred_element_type=jnp.float32)
        head_total = head_total + head_piece.astype(jnp.bfloat16).astype(jnp.float32)
    d_heads = head_total.astype(jnp.bfloat16)
    return d_hidden, d_heads
```

```python
import functools

import jax
import jax.numpy as jnp
from jax import lax
from jax.experimental import pallas as pl
from jax.experimental.pallas import tpu as pltpu
from jax.sharding import PartitionSpec as P

BF = jnp.bfloat16
F32 = jnp.float32
I32 = jnp.int32

ORDER = (0, 1, 7, 2, 6, 3, 5, 4)
NT = (((1,), (1,)), ((), ()))


def shift_x(value, step):
    pairs = [(4 * y + x, 4 * y + (x + step) % 4) for y in range(4) for x in range(4)]
    return lax.ppermute(value, "etp", pairs)


def shift_y(value, step):
    pairs = [(4 * y + x, 4 * ((y + step) % 4) + x) for y in range(4) for x in range(4)]
    return lax.ppermute(value, "etp", pairs)


def shift_z(value, step):
    pairs = []
    for low in range(4):
        for high in range(2):
            for core in range(2):
                to = (4 * high + low + step) % 8
                pairs.append((4 * low + 2 * high + core, 4 * (to % 4) + 2 * (to // 4) + core))
    return lax.ppermute(value, ("expert", "tp"), pairs)


def swap_core(value):
    return lax.ppermute(value, "tp", [(t, t ^ 1) for t in range(4)])


def dispatch_kernel(pos, ids, gates, grads, out0, out1, out2, out3, sel_out):
    outs = (out0, out1, out2, out3)
    expert = (lax.broadcasted_iota(I32, (8, 128), 0) + pos[0]) & 3
    hit0 = ids[0:1, :] == expert
    hit1 = ids[1:2, :] == expert
    zero = jnp.zeros((8, 128), F32)
    member = jnp.where(hit0 | hit1, 1.0, zero)
    weight = jnp.where(hit0, gates[0:1, :], zero) + jnp.where(hit1, gates[1:2, :], zero)
    before = lax.broadcasted_iota(I32, (128, 128), 0) < lax.broadcasted_iota(I32, (128, 128), 1)
    before = jnp.where(before, 1.0, jnp.zeros((128, 128), F32)).astype(BF)
    slot = jnp.dot(member.astype(BF), before, preferred_element_type=F32)
    slot_iota = lax.broadcasted_iota(I32, (64, 128), 0).astype(F32)
    for s in range(4):
        sel = jnp.where(slot[s : s + 1, :] == slot_iota, member[s : s + 1, :], 0.0)
        sel_bf = sel.astype(BF)
        rows = jnp.dot(sel_bf, grads[...], preferred_element_type=F32)
        row_weight = jnp.sum(sel * weight[s : s + 1, :], axis=1, keepdims=True)
        outs[s][...] = (rows * row_weight).astype(BF)
        sel_out[64 * s : 64 * (s + 1), :] = sel_bf


def dispatch(pos, ids, gates, grads):
    vm = pl.BlockSpec(memory_space=pltpu.VMEM)
    return pl.pallas_call(
        dispatch_kernel,
        in_specs=[pl.BlockSpec(memory_space=pltpu.SMEM), vm, vm, vm],
        out_specs=[vm] * 5,
        out_shape=[jax.ShapeDtypeStruct((64, 384), BF)] * 4 + [jax.ShapeDtypeStruct((256, 128), BF)],
        name="dispatch",
    )(pos, ids, gates, grads)


def combine_kernel(sel, grads, *refs):
    blocks, out = refs[:8], refs[8]
    rows = jnp.concatenate([b[...] for b in blocks], axis=0)
    both = jnp.concatenate([sel[...], sel[...]], axis=0)
    moe = lax.dot_general(both, rows, (((0,), (0,)), ((), ())), preferred_element_type=F32)
    out[...] = (grads[...].astype(F32) + moe).astype(BF)


def combine(sel, grads, blocks):
    return pl.pallas_call(
        combine_kernel,
        out_shape=jax.ShapeDtypeStruct((128, 384), BF),
        name="combine",
    )(sel, grads, *blocks)


def hold(segment, size=4):
    def index(i, idx):
        return (0, jnp.clip(i - size * segment, 0, size - 1))

    return index


def act_first_kernel(idx, *refs):
    pieces, weights, acc = refs[:12], refs[12:16], refs[16]
    step = pl.program_id(0)

    @pl.when(step == 0)
    def _():
        acc[...] = jnp.zeros_like(acc)

    for group in range(3):

        @pl.when(step // 4 == group)
        def _(group=group):
            for half in range(2):
                top, bottom = pieces[4 * group + 2 * half], pieces[4 * group + 2 * half + 1]
                rows = jnp.concatenate([top[...], bottom[...]], axis=0)
                for side in range(2):
                    acc[256 * half : 256 * (half + 1), 256 * side : 256 * (side + 1)] += lax.dot_general(
                        rows, weights[2 * half + side][...], NT, preferred_element_type=F32
                    )


def act_first(idx, pieces, down_own, down_other):
    piece_specs = [pl.BlockSpec((128, 384), hold(k // 4)) for k in range(12)]
    weight_a = pl.BlockSpec((256, 384), lambda i, idx: (0, idx[i]))
    weight_b = pl.BlockSpec((256, 384), lambda i, idx: (0, idx[12 + i]))
    return pl.pallas_call(
        act_first_kernel,
        grid_spec=pltpu.PrefetchScalarGridSpec(
            num_scalar_prefetch=1,
            grid=(12,),
            in_specs=piece_specs + [weight_a, weight_a, weight_b, weight_b],
            out_specs=pl.BlockSpec((512, 512), lambda i, idx: (0, 0)),
        ),
        out_shape=jax.ShapeDtypeStruct((512, 512), F32),
        name="act_first",
    )(idx, *pieces, down_own, down_other, down_own, down_other)


def act_last_kernel(idx, *refs):
    pieces, weights, acc_in = refs[:4], refs[4:8], refs[8]
    gates, ups, out, acc = refs[9:11], refs[11:13], refs[13], refs[14]
    step = pl.program_id(0)

    @pl.when(step == 0)
    def _():
        acc[...] = acc_in[...]

    for half in range(2):
        rows = jnp.concatenate([pieces[2 * half][...], pieces[2 * half + 1][...]], axis=0)
        for side in range(2):
            acc[256 * half : 256 * (half + 1), 256 * side : 256 * (side + 1)] += lax.dot_general(
                rows, weights[2 * half + side][...], NT, preferred_element_type=F32
            )

    @pl.when(step == 3)
    def _():
        for block in range(8):
            start = pl.multiple_of(idx[8 + block] * 64, 64)
            for side in range(2):
                gate = gates[side][pl.ds(start, 64), :].astype(F32)
                up = ups[side][pl.ds(start, 64), :].astype(F32)
                act = acc[64 * block : 64 * (block + 1), 256 * side : 256 * (side + 1)]
                sigma = 1.0 / (1.0 + jnp.exp(-gate))
                common = act * sigma
                out[64 * block : 64 * (block + 1), 256 * side : 256 * (side + 1)] = (
                    common * up * (1.0 + gate * (1.0 - sigma))
                ).astype(BF)
                out[64 * block : 64 * (block + 1), 512 + 256 * side : 512 + 256 * (side + 1)] = (
                    common * gate
                ).astype(BF)


def act_last(idx, pieces, down_own, down_other, acc, gate_own, gate_other, up_own, up_other):
    def whole(shape):
        return pl.BlockSpec(shape, lambda i, idx: (0, 0))

    piece_specs = [pl.BlockSpec((128, 384), hold(0)) for _ in range(4)]
    weight_a = pl.BlockSpec((256, 384), lambda i, idx: (0, idx[i]))
    weight_b = pl.BlockSpec((256, 384), lambda i, idx: (0, idx[4 + i]))
    return pl.pallas_call(
        act_last_kernel,
        grid_spec=pltpu.PrefetchScalarGridSpec(
            num_scalar_prefetch=1,
            grid=(4,),
            in_specs=piece_specs
            + [weight_a, weight_a, weight_b, weight_b, whole((512, 512))]
            + [whole((1024, 256))] * 4,
            out_specs=whole((512, 1024)),
            scratch_shapes=[pltpu.VMEM((512, 512), F32)],
        ),
        out_shape=jax.ShapeDtypeStruct((512, 1024), BF),
        name="act_last",
    )(idx, *pieces, down_own, down_other, down_own, down_other, acc, gate_own, gate_other, up_own, up_other)


def part_kernel(segments, split, idx, grads, gate_own, gate_other, up_own, up_other, *outs):
    step = pl.program_id(0)
    total = None
    for k, weight in enumerate((gate_own, gate_other, up_own, up_other)):
        term = lax.dot_general(
            grads[:, 256 * k : 256 * (k + 1)], weight[...], NT, preferred_element_type=F32
        )
        total = term if total is None else total + term
    for segment in range(len(segments)):

        @pl.when(step // 4 == segment)
        def _(segment=segment):
            if split:
                outs[2 * segment][...] = total[0:128].astype(BF)
                outs[2 * segment + 1][...] = total[128:256].astype(BF)
            else:
                outs[segment][...] = total


def parts(idx, grads, weights, segments, split, name):
    half_of = segments

    def grad_index(i, idx):
        return (idx[4 * len(half_of) + i // 4], 0)

    weight_spec = pl.BlockSpec((384, 256), lambda i, idx: (idx[i], 0))
    height = 128 if split else 256
    per = 2 if split else 1
    outs = per * len(segments)
    return pl.pallas_call(
        functools.partial(part_kernel, segments, split),
        grid_spec=pltpu.PrefetchScalarGridSpec(
            num_scalar_prefetch=1,
            grid=(4 * len(segments),),
            in_specs=[pl.BlockSpec((256, 1024), grad_index)] + [weight_spec] * 4,
            out_specs=[pl.BlockSpec((height, 384), hold(k // per)) for k in range(outs)],
        ),
        out_shape=[jax.ShapeDtypeStruct((height, 1536), BF if split else F32)] * outs,
        name=name,
    )(idx, grads, *weights)


def gather_first(own, shift):
    ahead = shift(own, -1)
    behind = shift(own, 1)
    far_top = shift(ahead[:128], -1)
    far_bottom = shift(behind[128:], 1)
    top = jnp.concatenate([own[:128], ahead[:128], far_top, behind[:128]], axis=1)
    bottom = jnp.concatenate([own[128:], ahead[128:], far_bottom, behind[128:]], axis=1)
    return top, bottom


def gather_second(top, bottom, shift):
    behind_bottom = shift(bottom, 1)
    ahead_top = shift(top, -1)
    behind_top = shift(top, 1)
    ahead_bottom = shift(bottom, -1)
    far_bottom = shift(behind_bottom, 1)
    far_top = shift(ahead_top, -1)
    return (ahead_top, ahead_bottom), (behind_top, behind_bottom), (far_top, far_bottom)


def add(*terms):
    total = terms[0].astype(F32)
    for term in terms[1:]:
        total = total + term.astype(F32)
    return total


def scatter_first(far, near, own, shift):
    far_top, far_bottom = far
    ahead_top, ahead_bottom, behind_top, behind_bottom = near
    got_top = shift(far_top, 1)
    got_bottom = shift(far_bottom, -1)
    from_behind_bottom = shift(ahead_bottom, 1)
    from_ahead_top = shift(behind_top, -1)
    from_behind_top = shift(add(ahead_top, got_top).astype(BF), 1)
    from_ahead_bottom = shift(add(behind_bottom, got_bottom).astype(BF), -1)
    top = add(own[:128], from_behind_top, from_ahead_top)
    bottom = add(own[128:], from_behind_bottom, from_ahead_bottom)
    return top, bottom


def scatter_second(top, bottom, shift):
    def chunk(half, j):
        return half[:, 384 * j : 384 * (j + 1)]

    got_top = shift(chunk(top, 2).astype(BF), 1)
    got_bottom = shift(chunk(bottom, 2).astype(BF), -1)
    to_ahead = jnp.concatenate([add(chunk(top, 1), got_top), chunk(bottom, 1)], axis=0).astype(BF)
    to_behind = jnp.concatenate([chunk(top, 3), add(chunk(bottom, 3), got_bottom)], axis=0).astype(BF)
    from_behind = shift(to_ahead, 1)
    from_ahead = shift(to_behind, -1)
    own = jnp.concatenate([chunk(top, 0), chunk(bottom, 0)], axis=0)
    return add(own, from_behind, from_ahead).astype(BF)


def body(d_out, expert_ids, gate_weights, saved_gate, saved_up, w_gate, w_up, w_down, w_out):
    expert = lax.axis_index("expert")
    etp = lax.axis_index("etp")
    tp = lax.axis_index("tp")
    y, x = etp // 4, etp % 4
    z = 4 * (tp // 2) + expert
    core = tp % 2

    def block_of(dy, dx):
        return 4 * ((y + dy) % 4) + (x + dx) % 4

    def run_a(dy):
        return [block_of(dy, j) for j in range(4)]

    def run_b(dx):
        return [block_of(j, dx) for j in range(4)]

    def source_block(step):
        place = (z - step) % 8
        return 4 * (place % 4) + 2 * (place // 4) + core

    def table(*entries):
        return jnp.stack([jnp.asarray(v, I32) for v in entries])

    sent = dispatch(jnp.reshape(expert, (1,)).astype(I32), expert_ids.T, gate_weights.T, d_out)
    sel = sent[4]

    down_own, gate_own, up_own = w_down[0], w_gate[0], w_up[0]
    saved_gate_own, saved_up_own = saved_gate[0], saved_up[0]

    blocks = [sent[0] if s == 0 else shift_z(sent[s % 4], s) for s in ORDER]
    rows_a = jnp.concatenate(blocks[:4], axis=0)
    rows_b = jnp.concatenate(blocks[4:], axis=0)

    down_other = swap_core(down_own)
    saved_gate_other = swap_core(saved_gate_own)
    saved_up_other = swap_core(saved_up_own)
    gate_other = swap_core(gate_own)
    up_other = swap_core(up_own)

    top_a, bottom_a = gather_first(rows_a, shift_x)
    top_b, bottom_b = gather_first(rows_b, shift_y)
    ahead_a, behind_a, far_a = gather_second(top_a, bottom_a, shift_y)
    ahead_b, behind_b, far_b = gather_second(top_b, bottom_b, shift_x)

    acc = act_first(
        table(*run_a(0), *run_a(1), *run_a(3), *run_b(0), *run_b(1), *run_b(3)),
        (top_a, bottom_a, top_b, bottom_b, *ahead_a, *ahead_b, *behind_a, *behind_b),
        down_own,
        down_other,
    )
    grads = act_last(
        table(*run_a(2), *run_b(2), *[source_block(s) for s in ORDER]),
        (*far_a, *far_b),
        down_own,
        down_other,
        acc,
        saved_gate_own,
        saved_gate_other,
        saved_up_own,
        saved_up_other,
    )

    weights = (gate_own, gate_other, up_own, up_other)
    far = parts(table(*run_a(2), *run_b(2), 0, 1), grads, weights, (0, 1), True, "part_far")
    near = parts(
        table(*run_a(1), *run_a(3), *run_b(1), *run_b(3), 0, 0, 1, 1),
        grads,
        weights,
        (0, 0, 1, 1),
        True,
        "part_near",
    )
    own = parts(table(*run_a(0), *run_b(0), 0, 1), grads, weights, (0, 1), False, "part_own")

    sum_a = scatter_first(far[0:2], near[0:4], own[0], shift_y)
    sum_b = scatter_first(far[2:4], near[4:8], own[1], shift_x)
    reduced_a = scatter_second(*sum_a, shift_x)
    reduced_b = scatter_second(*sum_b, shift_y)

    returned = [None] * 8
    for k, s in enumerate(ORDER):
        half = reduced_a if k < 4 else reduced_b
        rows = half[64 * (k % 4) : 64 * (k % 4 + 1)]
        returned[s] = rows if s == 0 else shift_z(rows, -s)
    d_hidden = combine(sel, d_out, returned)

    head_partial = lax.dot_general(
        lax.all_gather(d_hidden, "tp", axis=0, tiled=True), w_out, NT, preferred_element_type=F32
    ).astype(BF)
    spread = lax.all_to_all(head_partial.reshape(16, 32, 1536), "etp", 0, 0, tiled=True)
    d_heads = jnp.sum(spread.astype(F32), axis=0).astype(BF)
    return (d_hidden, d_heads)


def solution(mesh):
    in_specs = (
        P(("expert", "tp"), "etp"),
        P(("expert", "tp"), None),
        P(("expert", "tp"), None),
        P("expert", None, ("etp", "tp")),
        P("expert", None, ("etp", "tp")),
        P("expert", None, ("etp", "tp")),
        P("expert", None, ("etp", "tp")),
        P("expert", ("etp", "tp"), None),
        P("tp", "etp"),
    )
    out_specs = (P(("expert", "tp"), "etp"), P(("expert", "etp"), "tp"))
    return jax.shard_map(body, mesh=mesh, in_specs=in_specs, out_specs=out_specs, check_vma=False)
```

```python
import jax
import jax.numpy as jnp
from jax import lax
from jax.experimental import pallas as pl
from jax.experimental.pallas import tpu as pltpu
from jax.sharding import PartitionSpec as P

BF = jnp.bfloat16
F32 = jnp.float32
I32 = jnp.int32

NN = (((1,), (0,)), ((), ()))
NT = (((1,), (1,)), ((), ()))
VM = pl.BlockSpec(memory_space=pltpu.VMEM)
SM = pl.BlockSpec(memory_space=pltpu.SMEM)


def shape(dims, kind=BF):
    return jax.ShapeDtypeStruct(dims, kind)


def shift_plane(value, step, first):
    pairs = []
    for y in range(4):
        for x in range(4):
            for t in range(4):
                along_x = (t % 2 == 0) == first
                to_y = y if along_x else (y + step) % 4
                to_x = (x + step) % 4 if along_x else x
                pairs.append((16 * y + 4 * x + t, 16 * to_y + 4 * to_x + t))
    return lax.ppermute(value, ("etp", "tp"), pairs)


def shift_z(value, step):
    pairs = []
    for low in range(4):
        for high in range(2):
            for core in range(2):
                to = (4 * high + low + (step if core == 0 else -step)) % 8
                pairs.append((4 * low + 2 * high + core, 4 * (to % 4) + 2 * (to // 4) + core))
    return lax.ppermute(value, ("expert", "tp"), pairs)


def swap_core(value):
    return lax.ppermute(value, "tp", [(t, t ^ 1) for t in range(4)])


def dispatch_kernel(pos, ids, gates, grads, near, far, sel_out):
    expert = (pos[0] + pos[1] * lax.broadcasted_iota(I32, (8, 128), 0)) & 3
    hit0 = ids[0:1, :] == expert
    hit1 = ids[1:2, :] == expert
    zero = jnp.zeros((8, 128), F32)
    member = jnp.where(hit0 | hit1, 1.0, zero)
    weight = jnp.where(hit0, gates[0:1, :], zero) + jnp.where(hit1, gates[1:2, :], zero)
    before = lax.broadcasted_iota(I32, (128, 128), 0) < lax.broadcasted_iota(I32, (128, 128), 1)
    before = jnp.where(before, 1.0, jnp.zeros((128, 128), F32)).astype(BF)
    slot = jnp.dot(member.astype(BF), before, preferred_element_type=F32)
    slot_iota = lax.broadcasted_iota(I32, (64, 128), 0).astype(F32)
    for s in range(4):
        sel = jnp.where(slot[s : s + 1, :] == slot_iota, member[s : s + 1, :], 0.0)
        sel_bf = sel.astype(BF)
        rows = jnp.dot(sel_bf, grads[...], preferred_element_type=F32)
        row_weight = jnp.sum(sel * weight[s : s + 1, :], axis=1, keepdims=True)
        rows = (rows * row_weight).astype(BF)
        if s == 0:
            near[...] = rows
        else:
            far[64 * (s - 1) : 64 * s, :] = rows
        sel_out[64 * s : 64 * (s + 1), :] = sel_bf


def dispatch(pos, ids, gates, grads):
    return pl.pallas_call(
        dispatch_kernel,
        in_specs=[SM, VM, VM, VM],
        out_specs=[VM] * 3,
        out_shape=[shape((64, 384)), shape((192, 384)), shape((256, 128))],
        name="dispatch",
    )(pos, ids, gates, grads)


def combine_kernel(sel, grads, from1, from2, from3, other, own, across, out):
    rows = jnp.concatenate(
        [from1[0:64], from2[0:64], from3[0:64], other[...], own[...], across[...]], axis=0
    )
    order = (1, 2, 3, 3, 2, 1, 0, 0)
    picks = jnp.concatenate([sel[64 * k : 64 * (k + 1)] for k in order], axis=0)
    moe = lax.dot_general(picks, rows, (((0,), (0,)), ((), ())), preferred_element_type=F32)
    out[...] = (grads[...].astype(F32) + moe).astype(BF)


def combine(*args):
    return pl.pallas_call(combine_kernel, out_shape=shape((128, 384)), name="combine")(*args)


def factors_kernel(table, gate_own, gate_other, up_own, up_other, for_gate, for_up):
    for side, (gates, ups) in enumerate(((gate_own, up_own), (gate_other, up_other))):
        to_gate, to_up = [], []
        for block in range(8):
            start = pl.multiple_of(table[16 + block] * 64, 64)
            gate = gates[pl.ds(start, 64), :].astype(F32)
            up = ups[pl.ds(start, 64), :].astype(F32)
            sigma = 1.0 / (1.0 + jnp.exp(-gate))
            to_gate.append(up * sigma * (1.0 + gate * (1.0 - sigma)))
            to_up.append(gate * sigma)
        for_gate[256 * side : 256 * (side + 1), :] = jnp.concatenate(to_gate, axis=0).T
        for_up[256 * side : 256 * (side + 1), :] = jnp.concatenate(to_up, axis=0).T


def factors(table, *saved):
    return pl.pallas_call(
        factors_kernel,
        in_specs=[SM] + [VM] * 4,
        out_specs=[VM] * 2,
        out_shape=[shape((512, 512), F32)] * 2,
        name="factors",
    )(table, *saved)


def act_first_kernel(table, *refs):
    pieces, down_own, down_other, acc = refs[:6], refs[6], refs[7], refs[8]
    for k, group in enumerate((0, 1, 3)):
        rows = jnp.concatenate([pieces[2 * k][...], pieces[2 * k + 1][...]], axis=0)
        for side, down in enumerate((down_own, down_other)):
            columns = [
                down[:, pl.ds(pl.multiple_of(table[4 * group + j] * 384, 384), 384)] for j in range(4)
            ]
            term = lax.dot_general(
                jnp.concatenate(columns, axis=1), rows, NT, preferred_element_type=F32
            )
            if k == 0:
                acc[256 * side : 256 * (side + 1), :] = term
            else:
                acc[256 * side : 256 * (side + 1), :] += term


def act_first(table, pieces, down_own, down_other):
    return pl.pallas_call(
        act_first_kernel,
        in_specs=[SM] + [VM] * 8,
        out_specs=VM,
        out_shape=shape((512, 512), F32),
        name="act_first",
    )(table, *pieces, down_own, down_other)


def act_last_kernel(table, *refs):
    rows = jnp.concatenate([refs[0][...], refs[1][...]], axis=0)
    acc, for_gate, for_up, out = refs[10:14]
    for side in range(2):
        columns = jnp.concatenate([refs[2 + 4 * side + j][...] for j in range(4)], axis=1)
        here = slice(256 * side, 256 * (side + 1))
        act = acc[here, :] + lax.dot_general(columns, rows, NT, preferred_element_type=F32)
        out[256 * side : 256 * (side + 1), :] = (act * for_gate[here, :]).astype(BF)
        out[512 + 256 * side : 512 + 256 * (side + 1), :] = (act * for_up[here, :]).astype(BF)


def act_last(table, pieces, down_own, down_other, acc, for_gate, for_up):
    def column(j):
        return pl.BlockSpec((256, 384), lambda i, table: (0, table[8 + j]))

    def whole(dims):
        return pl.BlockSpec(dims, lambda i, table: (0, 0))

    columns = [column(j) for j in range(4)]
    return pl.pallas_call(
        act_last_kernel,
        grid_spec=pltpu.PrefetchScalarGridSpec(
            num_scalar_prefetch=1,
            grid=(1,),
            in_specs=[whole((256, 1536))] * 2 + columns * 2 + [whole((512, 512))] * 3,
            out_specs=whole((1024, 512)),
        ),
        out_shape=shape((1024, 512)),
        name="act_last",
    )(table, *pieces, *[down_own] * 4, *[down_other] * 4, acc, for_gate, for_up)


def part_kernel(table, *refs):
    weights, grads, top, bottom = refs[:8], refs[8], refs[9], refs[10]
    for j in range(2):
        total = None
        for k in range(4):
            term = lax.dot_general(
                weights[2 * k + j][...],
                grads[256 * k : 256 * (k + 1), :],
                NN,
                preferred_element_type=F32,
            )
            total = term if total is None else total + term
        top[384 * j : 384 * (j + 1), :] = total[:, 0:256].astype(BF)
        bottom[384 * j : 384 * (j + 1), :] = total[:, 256:512].astype(BF)


def part(table, grads, weights, group, name):
    def rows(j):
        return pl.BlockSpec((384, 256), lambda i, table: (table[4 * group + 2 * i + j], 0))

    half = pl.BlockSpec((768, 256), lambda i, table: (i, 0))
    return pl.pallas_call(
        part_kernel,
        grid_spec=pltpu.PrefetchScalarGridSpec(
            num_scalar_prefetch=1,
            grid=(2,),
            in_specs=[rows(0), rows(1)] * 4 + [pl.BlockSpec((1024, 512), lambda i, table: (0, 0))],
            out_specs=[half, half],
        ),
        out_shape=[shape((1536, 256))] * 2,
        name=name,
    )(table, *[w for weight in weights for w in (weight, weight)], grads)


def add(*terms):
    total = terms[0].astype(F32)
    for term in terms[1:]:
        total = total + term.astype(F32)
    return total


def pair_kernel(mine_a, got_a, mine_b, got_b, out_a, out_b):
    out_a[...] = add(mine_a[...], got_a[...]).astype(BF)
    out_b[...] = add(mine_b[...], got_b[...]).astype(BF)


def add_pairs(*args):
    return pl.pallas_call(pair_kernel, out_shape=[shape((1536, 256))] * 2, name="add_pairs")(*args)


def middle_kernel(own_t, own_b, t1, t2, b1, b2, far_top, far_bottom, ahead, behind, own):
    for j in range(4):
        here = slice(384 * j, 384 * (j + 1))
        top = add(own_t[here, :], t1[here, :], t2[here, :])
        bottom = add(own_b[here, :], b1[here, :], b2[here, :])
        if j == 2:
            far_top[...] = top.astype(BF)
            far_bottom[...] = bottom.astype(BF)
        else:
            out = {0: own, 1: ahead, 3: behind}[j]
            out[:, 0:256] = top
            out[:, 256:512] = bottom


def middle(*args):
    whole = shape((384, 512), F32)
    return pl.pallas_call(
        middle_kernel,
        out_shape=[shape((384, 256))] * 2 + [whole] * 3,
        name="middle",
    )(*args)


def second_kernel(ahead, behind, got_top, got_bottom, to_ahead, to_behind):
    to_ahead[:, 0:256] = add(ahead[:, 0:256], got_top[...]).astype(BF)
    to_ahead[:, 256:512] = ahead[:, 256:512].astype(BF)
    to_behind[:, 0:256] = behind[:, 0:256].astype(BF)
    to_behind[:, 256:512] = add(behind[:, 256:512], got_bottom[...]).astype(BF)


def second(*args):
    return pl.pallas_call(second_kernel, out_shape=[shape((384, 512))] * 2, name="second")(*args)


def last_kernel(own, got1, got2, back1, back2, back3, near, across):
    rows = add(own[...], got1[...], got2[...]).T.astype(BF)
    back1[...] = rows[0:128]
    back2[...] = rows[128:256]
    back3[...] = rows[256:384]
    near[...] = rows[384:448]
    across[...] = rows[448:512]


def last(*args):
    return pl.pallas_call(
        last_kernel,
        out_shape=[shape((128, 384))] * 3 + [shape((64, 384))] * 2,
        name="last",
    )(*args)


def body(d_out, expert_ids, gate_weights, saved_gate, saved_up, w_gate, w_up, w_down, w_out):
    expert = lax.axis_index("expert").astype(I32)
    etp = lax.axis_index("etp").astype(I32)
    tp = lax.axis_index("tp").astype(I32)
    y, x = etp // 4, etp % 4
    core = tp % 2
    z = 4 * (tp // 2) + expert
    direction = 1 - 2 * core

    i = jnp.arange(24, dtype=I32)
    d, j = i // 4, i % 4
    feature = 4 * ((y + jnp.where(core == 0, d, j)) % 4) + (x + jnp.where(core == 0, j, d)) % 4
    step = jnp.where(i >= 22, 4 * (i - 22), direction * ((i - 14) // 2))
    place = (z - step + 16) % 8
    source_core = jnp.where((i < 22) & (i % 2 == 1), 1 - core, core)
    table = jnp.where(i < 16, feature, 4 * (place % 4) + 2 * (place // 4) + source_core)
    pos = jnp.where(jnp.arange(2) == 0, expert, direction)

    near, far, sel = dispatch(pos, expert_ids.T, gate_weights.T, d_out)
    other = swap_core(far)
    across = shift_z(near, 4)
    received = [
        shift_z(jnp.concatenate([far[64 * k - 64 : 64 * k], other[192 - 64 * k : 256 - 64 * k]]), k)
        for k in (1, 2, 3)
    ]

    down_own, gate_own, up_own = w_down[0], w_gate[0], w_up[0]
    down_other = swap_core(down_own)
    saved_gate_other = swap_core(saved_gate[0])
    saved_up_other = swap_core(saved_up[0])
    gate_other = swap_core(gate_own)
    up_other = swap_core(up_own)
    for_gate, for_up = factors(table, saved_gate[0], saved_gate_other, saved_up[0], saved_up_other)

    rows = jnp.concatenate([*received, near, across], axis=0)
    ahead = shift_plane(rows, -1, True)
    behind = shift_plane(rows, 1, True)
    far_top = shift_plane(ahead[:256], -1, True)
    far_bottom = shift_plane(behind[256:], 1, True)
    top = jnp.concatenate([rows[:256], ahead[:256], far_top, behind[:256]], axis=1)
    bottom = jnp.concatenate([rows[256:], ahead[256:], far_bottom, behind[256:]], axis=1)

    behind_bottom = shift_plane(bottom, 1, False)
    ahead_top = shift_plane(top, -1, False)
    behind_top = shift_plane(top, 1, False)
    ahead_bottom = shift_plane(bottom, -1, False)
    far_bottom = shift_plane(behind_bottom, 1, False)
    far_top = shift_plane(ahead_top, -1, False)

    acc = act_first(
        table,
        (top, bottom, ahead_top, ahead_bottom, behind_top, behind_bottom),
        down_own,
        down_other,
    )
    grads = act_last(table, (far_top, far_bottom), down_own, down_other, acc, for_gate, for_up)

    weights = (gate_own, gate_other, up_own, up_other)
    far_top, far_bottom = part(table, grads, weights, 2, "part_far")
    got_top = shift_plane(far_top, 1, False)
    got_bottom = shift_plane(far_bottom, -1, False)
    ahead_top, ahead_bottom = part(table, grads, weights, 1, "part_ahead")
    from_behind_bottom = shift_plane(ahead_bottom, 1, False)
    behind_top, behind_bottom = part(table, grads, weights, 3, "part_behind")
    from_ahead_top = shift_plane(behind_top, -1, False)
    to_ahead, to_behind = add_pairs(ahead_top, got_top, behind_bottom, got_bottom)
    from_behind_top = shift_plane(to_ahead, 1, False)
    from_ahead_bottom = shift_plane(to_behind, -1, False)
    own_top, own_bottom = part(table, grads, weights, 0, "part_own")

    far_top, far_bottom, ahead, behind, own = middle(
        own_top,
        own_bottom,
        from_behind_top,
        from_ahead_top,
        from_behind_bottom,
        from_ahead_bottom,
    )
    got_top = shift_plane(far_top, 1, True)
    got_bottom = shift_plane(far_bottom, -1, True)
    to_ahead, to_behind = second(ahead, behind, got_top, got_bottom)
    from_behind = shift_plane(to_ahead, 1, True)
    from_ahead = shift_plane(to_behind, -1, True)
    *back, near, across = last(own, from_behind, from_ahead)

    back = [shift_z(rows, -k) for k, rows in zip((1, 2, 3), back)]
    across = shift_z(across, 4)
    other = swap_core(jnp.concatenate([rows[64:128] for rows in back], axis=0))
    d_hidden = combine(sel, d_out, *back, other, near, across)

    head_partial = lax.dot_general(
        lax.all_gather(d_hidden, "tp", axis=0, tiled=True), w_out, NT, preferred_element_type=F32
    ).astype(BF)
    spread = lax.all_to_all(head_partial.reshape(16, 32, 1536), "etp", 0, 0, tiled=True)
    d_heads = jnp.sum(spread.astype(F32), axis=0).astype(BF)
    return (d_hidden, d_heads)


def solution(mesh):
    in_specs = (
        P(("expert", "tp"), "etp"),
        P(("expert", "tp"), None),
        P(("expert", "tp"), None),
        P("expert", None, ("etp", "tp")),
        P("expert", None, ("etp", "tp")),
        P("expert", None, ("etp", "tp")),
        P("expert", None, ("etp", "tp")),
        P("expert", ("etp", "tp"), None),
        P("tp", "etp"),
    )
    out_specs = (P(("expert", "tp"), "etp"), P(("expert", "etp"), "tp"))
    return jax.shard_map(body, mesh=mesh, in_specs=in_specs, out_specs=out_specs, check_vma=False)
```

```python
import functools

import jax
import jax.numpy as jnp
from jax import lax
from jax.experimental import pallas as pl
from jax.experimental.pallas import tpu as pltpu
from jax.sharding import PartitionSpec as P


BF = jnp.bfloat16
F32 = jnp.float32
I32 = jnp.int32

NN = (((1,), (0,)), ((), ()))
NT = (((1,), (1,)), ((), ()))
VM = pl.BlockSpec(memory_space=pltpu.VMEM)
SM = pl.BlockSpec(memory_space=pltpu.SMEM)


CHUNKS = (0, 1, 3, 2)


def room(mib):
    return pltpu.CompilerParams(vmem_limit_bytes=mib << 20)


def shape(dims, kind=BF):
    return jax.ShapeDtypeStruct(dims, kind)


def shift_plane(value, step, first):
    pairs = []
    for y in range(4):
        for x in range(4):
            for t in range(4):
                along_x = (t % 2 == 0) == first
                to_y = y if along_x else (y + step) % 4
                to_x = (x + step) % 4 if along_x else x
                pairs.append((16 * y + 4 * x + t, 16 * to_y + 4 * to_x + t))
    return lax.ppermute(value, ("etp", "tp"), pairs)


def shift_z(value, step):
    pairs = []
    for low in range(4):
        for high in range(2):
            for core in range(2):
                to = (4 * high + low + (step if core == 0 else -step)) % 8
                pairs.append((4 * low + 2 * high + core, 4 * (to % 4) + 2 * (to // 4) + core))
    return lax.ppermute(value, ("expert", "tp"), pairs)


def swap_core(value):
    return lax.ppermute(value, "tp", [(t, t ^ 1) for t in range(4)])


def dispatch_kernel(pos, ids, gates, grads, near, far, sel_out):
    expert = (pos[0] + pos[1] * lax.broadcasted_iota(I32, (8, 128), 0)) & 3
    hit0 = ids[0:1, :] == expert
    hit1 = ids[1:2, :] == expert
    zero = jnp.zeros((8, 128), F32)
    member = jnp.where(hit0 | hit1, 1.0, zero)
    weight = jnp.where(hit0, gates[0:1, :], zero) + jnp.where(hit1, gates[1:2, :], zero)
    before = lax.broadcasted_iota(I32, (128, 128), 0) < lax.broadcasted_iota(I32, (128, 128), 1)
    before = jnp.where(before, 1.0, jnp.zeros((128, 128), F32)).astype(BF)
    slot = jnp.dot(member.astype(BF), before, preferred_element_type=F32)
    slot_iota = lax.broadcasted_iota(I32, (64, 128), 0).astype(F32)
    for s in range(4):
        sel = jnp.where(slot[s : s + 1, :] == slot_iota, member[s : s + 1, :], 0.0)
        sel_bf = sel.astype(BF)
        rows = jnp.dot(sel_bf, grads[...], preferred_element_type=F32)
        row_weight = jnp.sum(sel * weight[s : s + 1, :], axis=1, keepdims=True)
        rows = (rows * row_weight).astype(BF)
        if s == 0:
            near[...] = rows
        else:
            far[64 * (s - 1) : 64 * s, :] = rows
        sel_out[64 * s : 64 * (s + 1), :] = sel_bf


def dispatch(pos, ids, gates, grads):
    return pl.pallas_call(
        dispatch_kernel,
        in_specs=[SM, VM, VM, VM],
        out_specs=[VM] * 3,
        out_shape=[shape((64, 384)), shape((192, 384)), shape((256, 128))],
        name="dispatch",
        compiler_params=room(4),
    )(pos, ids, gates, grads)


def combine_kernel(sel, grads, from1, from2, from3, other, own, across, out):
    rows = jnp.concatenate(
        [from1[0:64], from2[0:64], from3[0:64], other[...], own[...], across[...]], axis=0
    )
    order = (1, 2, 3, 3, 2, 1, 0, 0)
    picks = jnp.concatenate([sel[64 * k : 64 * (k + 1)] for k in order], axis=0)
    moe = lax.dot_general(picks, rows, (((0,), (0,)), ((), ())), preferred_element_type=F32)
    out[...] = (grads[...].astype(F32) + moe).astype(BF)


def combine(*args):
    return pl.pallas_call(
        combine_kernel, out_shape=shape((128, 384)), name="combine", compiler_params=room(4)
    )(*args)


def factors_kernel(table, gates, ups, mine, theirs, to_gate, to_up):
    for side, out in enumerate((mine, theirs)):

        def block_step(block, carry, side=side):
            start = pl.multiple_of(table[16 + 8 * side + block] * 64, 64)
            here = pl.ds(pl.multiple_of(block * 64, 64), 64)
            gate = gates[pl.ds(start, 64), :].astype(F32)
            up = ups[pl.ds(start, 64), :].astype(F32)
            sigma = 1.0 / (1.0 + jnp.exp(-gate))
            to_gate[here, :] = up * sigma * (1.0 + gate * (1.0 - sigma))
            to_up[here, :] = gate * sigma
            return carry

        lax.fori_loop(0, 8, block_step, 0)
        out[0:256, :] = to_gate[...].T
        out[256:512, :] = to_up[...].T


def factors(table, *saved):
    return pl.pallas_call(
        factors_kernel,
        in_specs=[SM] + [VM] * 2,
        out_specs=[VM] * 2,
        out_shape=[shape((512, 512), F32)] * 2,
        scratch_shapes=[pltpu.VMEM((512, 256), F32)] * 2,
        name="factors",
        compiler_params=room(16),
    )(table, *saved)


def act_first_kernel(table, *refs):
    pieces, down_own, down_other, acc = refs[:9], refs[9], refs[10], refs[11]
    for k, group in enumerate((0, 1, 3)):
        top, bottom, far = pieces[3 * k : 3 * k + 3]
        rows = jnp.concatenate(
            [jnp.concatenate([top[...], bottom[...]], axis=0), far[...]], axis=1
        )
        for side, down in enumerate((down_own, down_other)):
            columns = [
                down[:, pl.ds(pl.multiple_of(table[4 * group + j] * 384, 384), 384)] for j in CHUNKS
            ]
            term = lax.dot_general(
                jnp.concatenate(columns, axis=1), rows, NT, preferred_element_type=F32
            )
            if k == 0:
                acc[256 * side : 256 * (side + 1), :] = term
            else:
                acc[256 * side : 256 * (side + 1), :] += term


def act_first(table, pieces, down_own, down_other):
    return pl.pallas_call(
        act_first_kernel,
        in_specs=[SM] + [VM] * 11,
        out_specs=VM,
        out_shape=shape((512, 512), F32),
        name="act_first",
        compiler_params=room(28),
    )(table, *pieces, down_own, down_other)


def act_last_kernel(table, *refs):
    rows = jnp.concatenate([refs[0][...], refs[1][...]], axis=0)
    acc, out = refs[10], refs[13]
    for side in range(2):
        columns = jnp.concatenate([refs[2 + 4 * side + j][...] for j in range(4)], axis=1)
        here = slice(256 * side, 256 * (side + 1))
        act = acc[here, :] + lax.dot_general(columns, rows, NT, preferred_element_type=F32)
        factor = refs[11 + side]
        out[256 * side : 256 * (side + 1), :] = (act * factor[0:256, :]).astype(BF)
        out[512 + 256 * side : 512 + 256 * (side + 1), :] = (act * factor[256:512, :]).astype(BF)


def act_last(table, pieces, down_own, down_other, acc, factor_own, factor_other):
    def column(j):
        return pl.BlockSpec((256, 384), lambda i, table: (0, table[8 + CHUNKS[j]]))

    def whole(dims):
        return pl.BlockSpec(dims, lambda i, table: (0, 0))

    columns = [column(j) for j in range(4)]
    return pl.pallas_call(
        act_last_kernel,
        grid_spec=pltpu.PrefetchScalarGridSpec(
            num_scalar_prefetch=1,
            grid=(1,),
            in_specs=[whole((256, 1536))] * 2 + columns * 2 + [whole((512, 512))] * 3,
            out_specs=whole((1024, 512)),
        ),
        out_shape=shape((1024, 512)),
        name="act_last",
        compiler_params=room(20),
    )(table, *pieces, *[down_own] * 4, *[down_other] * 4, acc, factor_own, factor_other)


def part_kernel(groups, per, table, *refs):
    weights, grads, outs = refs[: 4 * per], refs[4 * per], refs[4 * per + 1 :]
    step = pl.program_id(0)
    for j in range(per):
        weight = jnp.concatenate([weights[per * k + j][...] for k in range(4)], axis=1)
        total = lax.dot_general(weight, grads[...], NN, preferred_element_type=F32).astype(BF)
        for run, group in enumerate(groups):
            for piece in range(4 // per):
                chunk = per * piece + j

                @pl.when(step == 4 // per * run + piece)
                def _(total=total, run=run, group=group, chunk=chunk):
                    if chunk == 3 and group != 2:
                        outs[3 * run + 2][...] = total
                    else:
                        here = slice(384 * chunk, 384 * (chunk + 1))
                        outs[3 * run][here, :] = total[:, 0:256]
                        outs[3 * run + 1][here, :] = total[:, 256:512]


def part(table, grads, weights, groups, per):
    steps = 4 // per

    def rows(j):
        def index(i, table):
            place = per * (i % steps) + j
            chunk = jnp.where(place == 2, 3, jnp.where(place == 3, 2, place))
            group = groups[0] if len(groups) == 1 else jnp.where(i < steps, *groups)
            return (table[4 * group + chunk], 0)

        return pl.BlockSpec((384, 256), index)

    dims = []
    for group in groups:
        dims += [(1536, 256)] * 2 if group == 2 else [(1152, 256), (1152, 256), (384, 512)]
    return pl.pallas_call(
        functools.partial(part_kernel, groups, per),
        grid_spec=pltpu.PrefetchScalarGridSpec(
            num_scalar_prefetch=1,
            grid=(steps * len(groups),),
            in_specs=[rows(j) for j in range(per)] * 4
            + [pl.BlockSpec((1024, 512), lambda i, table: (0, 0))],
            out_specs=[pl.BlockSpec(d, lambda i, table: (0, 0)) for d in dims],
        ),
        out_shape=[shape(d) for d in dims],
        compiler_params=room(20),
    )(table, *[w for weight in weights for w in [weight] * per], grads)


def add(*terms):
    total = terms[0].astype(F32)
    for term in terms[1:]:
        total = total + term.astype(F32)
    return total


def pairs_kernel(near_a, far_a, got_a, near_b, far_b, got_b, out_near_a, out_far_a, out_near_b, out_far_b):
    def some_rows(k, carry):
        here = pl.ds(pl.multiple_of(k * 128, 128), 128)
        out_near_a[here, :] = add(near_a[here, :], got_a[here, :]).astype(BF)
        out_near_b[here, :] = add(near_b[here, :], got_b[here, :]).astype(BF)
        return carry

    lax.fori_loop(0, 9, some_rows, 0)
    out_far_a[:, 0:256] = add(far_a[:, 0:256], got_a[1152:1536, :]).astype(BF)
    out_far_a[:, 256:512] = far_a[:, 256:512]
    out_far_b[:, 0:256] = far_b[:, 0:256]
    out_far_b[:, 256:512] = add(far_b[:, 256:512], got_b[1152:1536, :]).astype(BF)


def add_pairs(*args):
    return pl.pallas_call(
        pairs_kernel,
        out_shape=[shape((1152, 256)), shape((384, 512))] * 2,
        name="add_pairs",
        compiler_params=room(16),
    )(*args)


def far_kernel(own, got1, got2, top, bottom):
    total = add(own[...], got1[...], got2[...]).astype(BF)
    top[...] = total[:, 0:256]
    bottom[...] = total[:, 256:512]


def middle_far(*args):
    return pl.pallas_call(
        far_kernel,
        out_shape=[shape((384, 256))] * 2,
        name="middle_far",
        compiler_params=room(6),
    )(*args)


def near_kernel(own_t, own_b, t1, t2, b1, b2, got_top, got_bottom, own, ahead, behind):
    for k, out in enumerate((own, ahead, behind)):

        def some_rows(r, carry, k=k, out=out):
            to = pl.ds(pl.multiple_of(r * 128, 128), 128)
            here = pl.ds(pl.multiple_of(384 * k + r * 128, 128), 128)
            top = add(own_t[here, :], t1[here, :], t2[here, :])
            bottom = add(own_b[here, :], b1[here, :], b2[here, :])
            if k == 1:
                top = top + got_top[to, :].astype(F32)
            if k == 2:
                bottom = bottom + got_bottom[to, :].astype(F32)
            out[to, 0:256] = top.astype(out.dtype)
            out[to, 256:512] = bottom.astype(out.dtype)
            return carry

        lax.fori_loop(0, 3, some_rows, 0)


def middle_near(*args):
    return pl.pallas_call(
        near_kernel,
        out_shape=[shape((384, 512), F32), shape((384, 512)), shape((384, 512))],
        name="middle_near",
        compiler_params=room(16),
    )(*args)


def last_kernel(own, got1, got2, back1, back2, back3, near, across):
    rows = add(own[...], got1[...], got2[...]).T.astype(BF)
    back1[...] = rows[0:128]
    back2[...] = rows[128:256]
    back3[...] = rows[256:384]
    near[...] = rows[384:448]
    across[...] = rows[448:512]


def last(*args):
    return pl.pallas_call(
        last_kernel,
        out_shape=[shape((128, 384))] * 3 + [shape((64, 384))] * 2,
        name="last",
        compiler_params=room(8),
    )(*args)


def heads_kernel(tokens, weights, out):
    def some_rows(k, carry):
        here = pl.ds(pl.multiple_of(k * 256, 256), 256)
        out[here, :] = lax.dot_general(
            tokens[here, :], weights[...], NT, preferred_element_type=F32
        ).astype(BF)
        return carry

    lax.fori_loop(0, 2, some_rows, 0)


def heads(*args):
    return pl.pallas_call(
        heads_kernel, out_shape=shape((512, 1536)), name="heads", compiler_params=room(12)
    )(*args)


def body(d_out, expert_ids, gate_weights, saved_gate, saved_up, w_gate, w_up, w_down, w_out):
    expert = lax.axis_index("expert").astype(I32)
    etp = lax.axis_index("etp").astype(I32)
    tp = lax.axis_index("tp").astype(I32)
    y, x = etp // 4, etp % 4
    core = tp % 2
    z = 4 * (tp // 2) + expert
    direction = 1 - 2 * core

    i = jnp.arange(32, dtype=I32)
    d, j, q = i // 4, i % 4, i % 8
    feature = 4 * ((y + jnp.where(core == 0, d, j)) % 4) + (x + jnp.where(core == 0, j, d)) % 4
    holder = jnp.where(i < 24, core, 1 - core)
    step = jnp.where(q >= 6, 4 * (q - 6), (1 - 2 * holder) * (q // 2 + 1))
    place = (z - step + 16) % 8
    source_core = jnp.where((q < 6) & (q % 2 == 1), 1 - holder, holder)
    table = jnp.where(i < 16, feature, 4 * (place % 4) + 2 * (place // 4) + source_core)
    pos = jnp.where(jnp.arange(2) == 0, expert, direction)

    near, far, sel = dispatch(pos, expert_ids.T, gate_weights.T, d_out)
    other = swap_core(far)
    across = shift_z(near, 4)
    received = [
        shift_z(jnp.concatenate([far[64 * k - 64 : 64 * k], other[192 - 64 * k : 256 - 64 * k]]), k)
        for k in (1, 2, 3)
    ]

    down_own, gate_own, up_own = w_down[0], w_gate[0], w_up[0]
    down_other = swap_core(down_own)
    gate_other = swap_core(gate_own)
    up_other = swap_core(up_own)
    factor_own, sent_factor = factors(table, saved_gate[0], saved_up[0])

    rows = jnp.concatenate([*received, near, across], axis=0)
    ahead = shift_plane(rows, -1, True)
    behind = shift_plane(rows, 1, True)
    top = jnp.concatenate([rows[:256], ahead[:256], behind[:256]], axis=1)
    bottom = jnp.concatenate([rows[256:], ahead[256:], behind[256:]], axis=1)
    top, bottom, sent_factor = lax.optimization_barrier((top, bottom, sent_factor))
    factor_other = swap_core(sent_factor)
    far_top = shift_plane(ahead[:256], -1, True)
    far_bottom = shift_plane(behind[256:], 1, True)
    far = jnp.concatenate([far_top, far_bottom], axis=0)

    behind_bottom = shift_plane(bottom, 1, False)
    ahead_top = shift_plane(top, -1, False)
    behind_far = shift_plane(far, 1, False)
    ahead_far = shift_plane(far, -1, False)
    behind_top = shift_plane(top, 1, False)
    ahead_bottom = shift_plane(bottom, -1, False)
    last_bottom = shift_plane(jnp.concatenate([behind_bottom, behind_far[256:]], axis=1), 1, False)
    last_top = shift_plane(jnp.concatenate([ahead_top, ahead_far[:256]], axis=1), -1, False)

    acc = act_first(
        table,
        (top, bottom, far, ahead_top, ahead_bottom, ahead_far, behind_top, behind_bottom, behind_far),
        down_own,
        down_other,
    )
    grads = act_last(table, (last_top, last_bottom), down_own, down_other, acc, factor_own, factor_other)

    weights = (gate_own, gate_other, up_own, up_other)
    far_top, far_bottom = part(table, grads, weights, (2,), 2)
    got_top = shift_plane(far_top, 1, False)
    got_bottom = shift_plane(far_bottom, -1, False)
    near_parts = part(table, grads, weights, (1, 3), 2)
    ahead_top, ahead_bottom, ahead_far, behind_top, behind_bottom, behind_far = near_parts
    from_behind_bottom = shift_plane(ahead_bottom, 1, False)
    from_ahead_top = shift_plane(behind_top, -1, False)
    own_top, own_bottom, own_far = part(table, grads, weights, (0,), 1)
    up_near, up_far, down_near, down_far = add_pairs(
        ahead_top, ahead_far, got_top, behind_bottom, behind_far, got_bottom
    )
    from_behind_far = shift_plane(up_far, 1, False)
    from_ahead_far = shift_plane(down_far, -1, False)
    from_behind_top = shift_plane(up_near, 1, False)
    from_ahead_bottom = shift_plane(down_near, -1, False)

    far_top, far_bottom = middle_far(own_far, from_behind_far, from_ahead_far)
    got_top = shift_plane(far_top, 1, True)
    got_bottom = shift_plane(far_bottom, -1, True)
    own, to_ahead, to_behind = middle_near(
        own_top,
        own_bottom,
        from_behind_top,
        from_ahead_top,
        from_behind_bottom,
        from_ahead_bottom,
        got_top,
        got_bottom,
    )
    from_behind = shift_plane(to_ahead, 1, True)
    from_ahead = shift_plane(to_behind, -1, True)
    *back, near, across = last(own, from_behind, from_ahead)

    across = shift_z(across, 4)
    back = [shift_z(rows, -k) for k, rows in zip((1, 2, 3), back)]
    other = swap_core(jnp.concatenate([rows[64:128] for rows in back], axis=0))
    d_hidden = combine(sel, d_out, *back, other, near, across)

    head_partial = heads(lax.all_gather(d_hidden, "tp", axis=0, tiled=True), w_out)
    spread = lax.all_to_all(head_partial.reshape(16, 32, 1536), "etp", 0, 0, tiled=True)
    d_heads = jnp.sum(spread.astype(F32), axis=0).astype(BF)
    return (d_hidden, d_heads)


def solution(mesh):
    in_specs = (
        P(("expert", "tp"), "etp"),
        P(("expert", "tp"), None),
        P(("expert", "tp"), None),
        P("expert", None, ("etp", "tp")),
        P("expert", None, ("etp", "tp")),
        P("expert", None, ("etp", "tp")),
        P("expert", None, ("etp", "tp")),
        P("expert", ("etp", "tp"), None),
        P("tp", "etp"),
    )
    out_specs = (P(("expert", "tp"), "etp"), P(("expert", "etp"), "tp"))

    return jax.shard_map(body, mesh=mesh, in_specs=in_specs, out_specs=out_specs, check_vma=False)
```

```python
import functools

import jax
import jax.numpy as jnp
from jax import lax
from jax.experimental import pallas as pl
from jax.experimental.pallas import tpu as pltpu
from jax.sharding import PartitionSpec as P


BF = jnp.bfloat16
F32 = jnp.float32
I32 = jnp.int32

NN = (((1,), (0,)), ((), ()))
NT = (((1,), (1,)), ((), ()))
VM = pl.BlockSpec(memory_space=pltpu.VMEM)
SM = pl.BlockSpec(memory_space=pltpu.SMEM)


CHUNKS = (0, 1, 3, 2)


def room(mib):
    return pltpu.CompilerParams(vmem_limit_bytes=mib << 20)


def shape(dims, kind=BF):
    return jax.ShapeDtypeStruct(dims, kind)


def shift_plane(value, step, first):
    pairs = []
    for y in range(4):
        for x in range(4):
            for t in range(4):
                along_x = (t % 2 == 0) == first
                to_y = y if along_x else (y + step) % 4
                to_x = (x + step) % 4 if along_x else x
                pairs.append((16 * y + 4 * x + t, 16 * to_y + 4 * to_x + t))
    return lax.ppermute(value, ("etp", "tp"), pairs)


def shift_z(value, step):
    pairs = []
    for low in range(4):
        for high in range(2):
            for core in range(2):
                to = (4 * high + low + (step if core == 0 else -step)) % 8
                pairs.append((4 * low + 2 * high + core, 4 * (to % 4) + 2 * (to // 4) + core))
    return lax.ppermute(value, ("expert", "tp"), pairs)


def swap_core(value):
    return lax.ppermute(value, "tp", [(t, t ^ 1) for t in range(4)])


def dispatch_kernel(pos, ids, gates, grads, near, far, sel_out):
    expert = (pos[0] + pos[1] * lax.broadcasted_iota(I32, (8, 128), 0)) & 3
    hit0 = ids[0:1, :] == expert
    hit1 = ids[1:2, :] == expert
    zero = jnp.zeros((8, 128), F32)
    member = jnp.where(hit0 | hit1, 1.0, zero)
    weight = jnp.where(hit0, gates[0:1, :], zero) + jnp.where(hit1, gates[1:2, :], zero)
    before = lax.broadcasted_iota(I32, (128, 128), 0) < lax.broadcasted_iota(I32, (128, 128), 1)
    before = jnp.where(before, 1.0, jnp.zeros((128, 128), F32)).astype(BF)
    slot = jnp.dot(member.astype(BF), before, preferred_element_type=F32)
    slot_iota = lax.broadcasted_iota(I32, (64, 128), 0).astype(F32)
    for s in range(4):
        sel = jnp.where(slot[s : s + 1, :] == slot_iota, member[s : s + 1, :], 0.0)
        sel_bf = sel.astype(BF)
        rows = jnp.dot(sel_bf, grads[...], preferred_element_type=F32)
        row_weight = jnp.sum(sel * weight[s : s + 1, :], axis=1, keepdims=True)
        rows = (rows * row_weight).astype(BF)
        if s == 0:
            near[...] = rows
        else:
            far[64 * (s - 1) : 64 * s, :] = rows
        sel_out[64 * s : 64 * (s + 1), :] = sel_bf


def dispatch(pos, ids, gates, grads):
    return pl.pallas_call(
        dispatch_kernel,
        in_specs=[SM, VM, VM, VM],
        out_specs=[VM] * 3,
        out_shape=[shape((64, 384)), shape((192, 384)), shape((256, 128))],
        name="dispatch",
    )(pos, ids, gates, grads)


def combine_kernel(sel, grads, from1, from2, from3, other, own, across, out):
    rows = jnp.concatenate(
        [from1[0:64], from2[0:64], from3[0:64], other[...], own[...], across[...]], axis=0
    )
    order = (1, 2, 3, 3, 2, 1, 0, 0)
    picks = jnp.concatenate([sel[64 * k : 64 * (k + 1)] for k in order], axis=0)
    moe = lax.dot_general(picks, rows, (((0,), (0,)), ((), ())), preferred_element_type=F32)
    out[...] = (grads[...].astype(F32) + moe).astype(BF)


def combine(*args):
    return pl.pallas_call(
        combine_kernel, out_shape=shape((128, 384)), name="combine", compiler_params=room(4)
    )(*args)


def factors_kernel(table, gates, ups, mine, theirs, to_gate, to_up):
    for side, out in enumerate((mine, theirs)):

        def block_step(block, carry, side=side):
            start = pl.multiple_of(table[16 + 8 * side + block] * 64, 64)
            here = pl.ds(pl.multiple_of(block * 64, 64), 64)
            gate = gates[pl.ds(start, 64), :].astype(F32)
            up = ups[pl.ds(start, 64), :].astype(F32)
            sigma = 1.0 / (1.0 + jnp.exp(-gate))
            to_gate[here, :] = up * sigma * (1.0 + gate * (1.0 - sigma))
            to_up[here, :] = gate * sigma
            return carry

        lax.fori_loop(0, 8, block_step, 0)
        out[0:256, :] = to_gate[...].T
        out[256:512, :] = to_up[...].T


def factors(table, *saved):
    return pl.pallas_call(
        factors_kernel,
        in_specs=[SM] + [VM] * 2,
        out_specs=[VM] * 2,
        out_shape=[shape((512, 512), F32)] * 2,
        scratch_shapes=[pltpu.VMEM((512, 256), F32)] * 2,
        name="factors",
        compiler_params=room(16),
    )(table, *saved)


def pack_kernel(*refs):
    start = 0
    for ref in refs[:-1]:
        refs[-1][start : start + ref.shape[0], :] = ref[...]
        start += ref.shape[0]


def pack(*blocks):
    return pl.pallas_call(
        pack_kernel, out_shape=shape((512, 384)), name="pack", compiler_params=room(4)
    )(*blocks)


def beside_kernel(*refs):
    for k in range(3):
        refs[3][:, 384 * k : 384 * (k + 1)] = refs[k][...]


def beside(*blocks):
    return pl.pallas_call(
        beside_kernel, out_shape=shape((512, 1152)), name="beside", compiler_params=room(6)
    )(*blocks)


def halves_kernel(near_a, far_a, near_b, far_b, top, bottom):
    top[:, 0:1152] = near_a[0:256, :]
    top[:, 1152:1536] = far_a[0:256, :]
    bottom[:, 0:1152] = near_b[256:512, :]
    bottom[:, 1152:1536] = far_b[256:512, :]


def halves(*args):
    return pl.pallas_call(
        halves_kernel, out_shape=[shape((256, 1536))] * 2, name="halves", compiler_params=room(8)
    )(*args)


def act_first_kernel(table, *refs):
    pieces, down_own, down_other, acc = refs[:6], refs[6], refs[7], refs[8]
    for k, group in enumerate((0, 1, 3)):
        rows = jnp.concatenate([pieces[2 * k][...], pieces[2 * k + 1][...]], axis=1)
        for side, down in enumerate((down_own, down_other)):
            columns = [
                down[:, pl.ds(pl.multiple_of(table[4 * group + j] * 384, 384), 384)] for j in CHUNKS
            ]
            term = lax.dot_general(
                jnp.concatenate(columns, axis=1), rows, NT, preferred_element_type=F32
            )
            if k == 0:
                acc[256 * side : 256 * (side + 1), :] = term
            else:
                acc[256 * side : 256 * (side + 1), :] += term


def act_first(table, pieces, down_own, down_other):
    return pl.pallas_call(
        act_first_kernel,
        in_specs=[SM] + [VM] * 8,
        out_specs=VM,
        out_shape=shape((512, 512), F32),
        name="act_first",
        compiler_params=room(28),
    )(table, *pieces, down_own, down_other)


def act_last_kernel(table, *refs):
    rows = jnp.concatenate([refs[0][...], refs[1][...]], axis=0)
    acc, out = refs[10], refs[13]
    for side in range(2):
        columns = jnp.concatenate([refs[2 + 4 * side + j][...] for j in range(4)], axis=1)
        here = slice(256 * side, 256 * (side + 1))
        act = acc[here, :] + lax.dot_general(columns, rows, NT, preferred_element_type=F32)
        factor = refs[11 + side]
        out[256 * side : 256 * (side + 1), :] = (act * factor[0:256, :]).astype(BF)
        out[512 + 256 * side : 512 + 256 * (side + 1), :] = (act * factor[256:512, :]).astype(BF)


def act_last(table, pieces, down_own, down_other, acc, factor_own, factor_other):
    def column(j):
        return pl.BlockSpec((256, 384), lambda i, table: (0, table[8 + CHUNKS[j]]))

    def whole(dims):
        return pl.BlockSpec(dims, lambda i, table: (0, 0))

    columns = [column(j) for j in range(4)]
    return pl.pallas_call(
        act_last_kernel,
        grid_spec=pltpu.PrefetchScalarGridSpec(
            num_scalar_prefetch=1,
            grid=(1,),
            in_specs=[whole((256, 1536))] * 2 + columns * 2 + [whole((512, 512))] * 3,
            out_specs=whole((1024, 512)),
        ),
        out_shape=shape((1024, 512)),
        name="act_last",
        compiler_params=room(20),
    )(table, *pieces, *[down_own] * 4, *[down_other] * 4, acc, factor_own, factor_other)


def part_kernel(groups, per, table, *refs):
    weights, grads, outs = refs[: 4 * per], refs[4 * per], refs[4 * per + 1 :]
    step = pl.program_id(0)
    for j in range(per):
        weight = jnp.concatenate([weights[per * k + j][...] for k in range(4)], axis=1)
        total = lax.dot_general(weight, grads[...], NN, preferred_element_type=F32).astype(BF)
        for run, group in enumerate(groups):
            for piece in range(4 // per):
                chunk = per * piece + j

                @pl.when(step == 4 // per * run + piece)
                def _(total=total, run=run, group=group, chunk=chunk):
                    here = slice(384 * chunk, 384 * (chunk + 1))
                    if group == 2:
                        outs[0][here, :] = total[:, 0:256]
                        outs[1][here, :] = total[:, 256:512]
                    elif chunk == 3:
                        outs[2 * run + 1][...] = total
                    else:
                        outs[2 * run][here, :] = total


def part(table, grads, weights, groups, per):
    steps = 4 // per

    def rows(j):
        def index(i, table):
            place = per * (i % steps) + j
            chunk = jnp.where(place == 2, 3, jnp.where(place == 3, 2, place))
            group = groups[0] if len(groups) == 1 else jnp.where(i < steps, *groups)
            return (table[4 * group + chunk], 0)

        return pl.BlockSpec((384, 256), index)

    dims = []
    for group in groups:
        dims += [(1536, 256)] * 2 if group == 2 else [(1152, 512), (384, 512)]
    return pl.pallas_call(
        functools.partial(part_kernel, groups, per),
        grid_spec=pltpu.PrefetchScalarGridSpec(
            num_scalar_prefetch=1,
            grid=(steps * len(groups),),
            in_specs=[rows(j) for j in range(per)] * 4
            + [pl.BlockSpec((1024, 512), lambda i, table: (0, 0))],
            out_specs=[pl.BlockSpec(d, lambda i, table: (0, 0)) for d in dims],
        ),
        out_shape=[shape(d) for d in dims],
        compiler_params=room(20),
    )(table, *[w for weight in weights for w in [weight] * per], grads)


def add(*terms):
    total = terms[0].astype(F32)
    for term in terms[1:]:
        total = total + term.astype(F32)
    return total


def pairs_kernel(near_a, far_a, got_a, near_b, far_b, got_b, out_near_a, out_far_a, out_near_b, out_far_b):
    def some_rows(k, carry):
        here = pl.ds(pl.multiple_of(k * 128, 128), 128)
        out_near_a[here, 0:256] = add(near_a[here, 0:256], got_a[here, :]).astype(BF)
        out_near_a[here, 256:512] = near_a[here, 256:512]
        out_near_b[here, 0:256] = near_b[here, 0:256]
        out_near_b[here, 256:512] = add(near_b[here, 256:512], got_b[here, :]).astype(BF)
        return carry

    lax.fori_loop(0, 9, some_rows, 0)
    out_far_a[:, 0:256] = add(far_a[:, 0:256], got_a[1152:1536, :]).astype(BF)
    out_far_a[:, 256:512] = far_a[:, 256:512]
    out_far_b[:, 0:256] = far_b[:, 0:256]
    out_far_b[:, 256:512] = add(far_b[:, 256:512], got_b[1152:1536, :]).astype(BF)


def add_pairs(*args):
    return pl.pallas_call(
        pairs_kernel,
        out_shape=[shape((1152, 512)), shape((384, 512))] * 2,
        name="add_pairs",
        compiler_params=room(16),
    )(*args)


def far_kernel(own, got1, got2, out):
    out[...] = add(own[...], got1[...], got2[...]).astype(BF)


def middle_far(*args):
    return pl.pallas_call(
        far_kernel, out_shape=shape((384, 512)), name="middle_far", compiler_params=room(6)
    )(*args)


def near_kernel(mine, got1, got2, far, own, ahead, behind):
    for k, out in enumerate((own, ahead, behind)):

        def some_rows(r, carry, k=k, out=out):
            to = pl.ds(pl.multiple_of(r * 128, 128), 128)
            here = pl.ds(pl.multiple_of(384 * k + r * 128, 128), 128)
            total = add(mine[here, :], got1[here, :], got2[here, :])
            if k == 1:
                total = total + far[to, :].astype(F32)
            out[to, :] = total.astype(out.dtype)
            return carry

        lax.fori_loop(0, 3, some_rows, 0)


def middle_near(*args):
    return pl.pallas_call(
        near_kernel,
        out_shape=[shape((384, 512), F32), shape((384, 512)), shape((384, 512))],
        name="middle_near",
        compiler_params=room(16),
    )(*args)


def last_kernel(own, got1, got2, back1, back2, back3, near, across):
    rows = add(own[...], got1[...], got2[...]).T.astype(BF)
    back1[...] = rows[0:128]
    back2[...] = rows[128:256]
    back3[...] = rows[256:384]
    near[...] = rows[384:448]
    across[...] = rows[448:512]


def last(*args):
    return pl.pallas_call(
        last_kernel,
        out_shape=[shape((128, 384))] * 3 + [shape((64, 384))] * 2,
        name="last",
        compiler_params=room(8),
    )(*args)


def heads_kernel(tokens, weights, out):
    def some_rows(k, carry):
        here = pl.ds(pl.multiple_of(k * 256, 256), 256)
        out[here, :] = lax.dot_general(
            tokens[here, :], weights[...], NT, preferred_element_type=F32
        ).astype(BF)
        return carry

    lax.fori_loop(0, 2, some_rows, 0)


def heads(*args):
    return pl.pallas_call(
        heads_kernel, out_shape=shape((512, 1536)), name="heads", compiler_params=room(12)
    )(*args)


def body(d_out, expert_ids, gate_weights, saved_gate, saved_up, w_gate, w_up, w_down, w_out):
    expert = lax.axis_index("expert").astype(I32)
    etp = lax.axis_index("etp").astype(I32)
    tp = lax.axis_index("tp").astype(I32)
    y, x = etp // 4, etp % 4
    core = tp % 2
    z = 4 * (tp // 2) + expert
    direction = 1 - 2 * core

    i = jnp.arange(32, dtype=I32)
    d, j, q = i // 4, i % 4, i % 8
    feature = 4 * ((y + jnp.where(core == 0, d, j)) % 4) + (x + jnp.where(core == 0, j, d)) % 4
    holder = jnp.where(i < 24, core, 1 - core)
    step = jnp.where(q >= 6, 4 * (q - 6), (1 - 2 * holder) * (q // 2 + 1))
    place = (z - step + 16) % 8
    source_core = jnp.where((q < 6) & (q % 2 == 1), 1 - holder, holder)
    table = jnp.where(i < 16, feature, 4 * (place % 4) + 2 * (place // 4) + source_core)
    pos = jnp.where(jnp.arange(2) == 0, expert, direction)

    near, far, sel = dispatch(pos, expert_ids.T, gate_weights.T, d_out)
    other = swap_core(far)
    across = shift_z(near, 4)
    received = [
        shift_z(jnp.concatenate([far[64 * k - 64 : 64 * k], other[192 - 64 * k : 256 - 64 * k]]), k)
        for k in (1, 2, 3)
    ]

    down_own, gate_own, up_own = w_down[0], w_gate[0], w_up[0]
    down_other = swap_core(down_own)
    gate_other = swap_core(gate_own)
    up_other = swap_core(up_own)
    factor_own, sent_factor = factors(table, saved_gate[0], saved_up[0])

    rows = pack(*received, near, across)
    ahead = shift_plane(rows, -1, True)
    behind = shift_plane(rows, 1, True)
    near, sent_factor = lax.optimization_barrier((beside(rows, ahead, behind), sent_factor))
    factor_other = swap_core(sent_factor)
    far = shift_plane(ahead, -1, True)

    behind_near = shift_plane(near, 1, False)
    ahead_near = shift_plane(near, -1, False)
    behind_far = shift_plane(far, 1, False)
    ahead_far = shift_plane(far, -1, False)
    top, bottom = halves(ahead_near, ahead_far, behind_near, behind_far)
    last_top = shift_plane(top, -1, False)
    last_bottom = shift_plane(bottom, 1, False)

    acc = act_first(
        table,
        (near, far, ahead_near, ahead_far, behind_near, behind_far),
        down_own,
        down_other,
    )
    grads = act_last(table, (last_top, last_bottom), down_own, down_other, acc, factor_own, factor_other)

    weights = (gate_own, gate_other, up_own, up_other)
    far_top, far_bottom = part(table, grads, weights, (2,), 2)
    got_top = shift_plane(far_top, 1, False)
    got_bottom = shift_plane(far_bottom, -1, False)
    ahead_near, ahead_far, behind_near, behind_far = part(table, grads, weights, (1, 3), 2)
    own_near, own_far = part(table, grads, weights, (0,), 1)
    up_near, up_far, down_near, down_far = add_pairs(
        ahead_near, ahead_far, got_top, behind_near, behind_far, got_bottom
    )
    from_behind_far = shift_plane(up_far, 1, False)
    from_ahead_far = shift_plane(down_far, -1, False)
    from_behind_near = shift_plane(up_near, 1, False)
    from_ahead_near = shift_plane(down_near, -1, False)

    got_far = shift_plane(middle_far(own_far, from_behind_far, from_ahead_far), 1, True)
    own, to_ahead, to_behind = middle_near(own_near, from_behind_near, from_ahead_near, got_far)
    from_behind = shift_plane(to_ahead, 1, True)
    from_ahead = shift_plane(to_behind, -1, True)
    *back, near, across = last(own, from_behind, from_ahead)

    across = shift_z(across, 4)
    back = [shift_z(rows, -k) for k, rows in zip((1, 2, 3), back)]
    other = swap_core(jnp.concatenate([rows[64:128] for rows in back], axis=0))
    d_hidden = combine(sel, d_out, *back, other, near, across)

    head_partial = heads(lax.all_gather(d_hidden, "tp", axis=0, tiled=True), w_out)
    spread = lax.all_to_all(head_partial.reshape(16, 32, 1536), "etp", 0, 0, tiled=True)
    d_heads = jnp.sum(spread.astype(F32), axis=0).astype(BF)
    return (d_hidden, d_heads)


def solution(mesh):
    in_specs = (
        P(("expert", "tp"), "etp"),
        P(("expert", "tp"), None),
        P(("expert", "tp"), None),
        P("expert", None, ("etp", "tp")),
        P("expert", None, ("etp", "tp")),
        P("expert", None, ("etp", "tp")),
        P("expert", None, ("etp", "tp")),
        P("expert", ("etp", "tp"), None),
        P("tp", "etp"),
    )
    out_specs = (P(("expert", "tp"), "etp"), P(("expert", "etp"), "tp"))

    return jax.shard_map(body, mesh=mesh, in_specs=in_specs, out_specs=out_specs, check_vma=False)
```

```python
import functools

import jax
import jax.numpy as jnp
from jax import lax
from jax.experimental import pallas as pl
from jax.experimental.pallas import tpu as pltpu
from jax.sharding import PartitionSpec as P


BF = jnp.bfloat16
F32 = jnp.float32
I32 = jnp.int32

NN = (((1,), (0,)), ((), ()))
NT = (((1,), (1,)), ((), ()))
VM = pl.BlockSpec(memory_space=pltpu.VMEM)
SM = pl.BlockSpec(memory_space=pltpu.SMEM)


CHUNKS = (0, 1, 3, 2)


def room(mib):
    return pltpu.CompilerParams(vmem_limit_bytes=mib << 20)


def shape(dims, kind=BF):
    return jax.ShapeDtypeStruct(dims, kind)


def shift_plane(value, step, first):
    pairs = []
    for y in range(4):
        for x in range(4):
            for t in range(4):
                along_x = (t % 2 == 0) == first
                to_y = y if along_x else (y + step) % 4
                to_x = (x + step) % 4 if along_x else x
                pairs.append((16 * y + 4 * x + t, 16 * to_y + 4 * to_x + t))
    return lax.ppermute(value, ("etp", "tp"), pairs)


def shift_z(value, step):
    pairs = []
    for low in range(4):
        for high in range(2):
            for core in range(2):
                to = (4 * high + low + (step if core == 0 else -step)) % 8
                pairs.append((4 * low + 2 * high + core, 4 * (to % 4) + 2 * (to // 4) + core))
    return lax.ppermute(value, ("expert", "tp"), pairs)


def swap_core(value):
    return lax.ppermute(value, "tp", [(t, t ^ 1) for t in range(4)])


def dispatch_kernel(table, ids, gates, grads, near, far1, far2, far3, far, sel_out):
    expert = (table[32] + table[33] * lax.broadcasted_iota(I32, (8, 128), 0)) & 3
    hit0 = ids[0:1, :] == expert
    hit1 = ids[1:2, :] == expert
    zero = jnp.zeros((8, 128), F32)
    member = jnp.where(hit0 | hit1, 1.0, zero)
    weight = jnp.where(hit0, gates[0:1, :], zero) + jnp.where(hit1, gates[1:2, :], zero)
    before = lax.broadcasted_iota(I32, (128, 128), 0) < lax.broadcasted_iota(I32, (128, 128), 1)
    before = jnp.where(before, 1.0, jnp.zeros((128, 128), F32)).astype(BF)
    slot = jnp.dot(member.astype(BF), before, preferred_element_type=F32)
    slot_iota = lax.broadcasted_iota(I32, (64, 128), 0).astype(F32)
    for s in range(4):
        sel = jnp.where(slot[s : s + 1, :] == slot_iota, member[s : s + 1, :], 0.0)
        sel_bf = sel.astype(BF)
        rows = jnp.dot(sel_bf, grads[...], preferred_element_type=F32)
        row_weight = jnp.sum(sel * weight[s : s + 1, :], axis=1, keepdims=True)
        rows = (rows * row_weight).astype(BF)
        if s == 0:
            near[...] = rows
        else:
            far[64 * (s - 1) : 64 * s, :] = rows
            (far1, far2, far3)[s - 1][...] = rows
        sel_out[64 * s : 64 * (s + 1), :] = sel_bf


def dispatch(table, ids, gates, grads):
    return pl.pallas_call(
        dispatch_kernel,
        in_specs=[SM, VM, VM, VM],
        out_specs=[VM] * 6,
        out_shape=[shape((64, 384))] * 4 + [shape((192, 384)), shape((256, 128))],
        name="dispatch",
    )(table, ids, gates, grads)


def combine_kernel(sel, grads, from1, from2, from3, other, own, across, out):
    rows = jnp.concatenate(
        [from1[0:64], from2[0:64], from3[0:64], other[...], own[...], across[...]], axis=0
    )
    order = (1, 2, 3, 3, 2, 1, 0, 0)
    picks = jnp.concatenate([sel[64 * k : 64 * (k + 1)] for k in order], axis=0)
    moe = lax.dot_general(picks, rows, (((0,), (0,)), ((), ())), preferred_element_type=F32)
    out[...] = (grads[...].astype(F32) + moe).astype(BF)


def combine(*args):
    return pl.pallas_call(
        combine_kernel, out_shape=shape((128, 384)), name="combine", compiler_params=room(4)
    )(*args)


def factors_kernel(table, gates, ups, mine, theirs, to_gate, to_up):
    for side, out in enumerate((mine, theirs)):

        def block_step(block, carry, side=side):
            start = pl.multiple_of(table[16 + 8 * side + block] * 64, 64)
            here = pl.ds(pl.multiple_of(block * 64, 64), 64)
            gate = gates[pl.ds(start, 64), :].astype(F32)
            up = ups[pl.ds(start, 64), :].astype(F32)
            sigma = 1.0 / (1.0 + jnp.exp(-gate))
            to_gate[here, :] = up * sigma * (1.0 + gate * (1.0 - sigma))
            to_up[here, :] = gate * sigma
            return carry

        lax.fori_loop(0, 8, block_step, 0)
        out[0:256, :] = to_gate[...].T
        out[256:512, :] = to_up[...].T


def factors(table, *saved):
    return pl.pallas_call(
        factors_kernel,
        in_specs=[SM] + [VM] * 2,
        out_specs=[VM] * 2,
        out_shape=[shape((512, 512), F32)] * 2,
        scratch_shapes=[pltpu.VMEM((512, 256), F32)] * 2,
        name="factors",
        compiler_params=room(16),
    )(table, *saved)


def pack_kernel(*refs):
    start = 0
    for ref in refs[:-1]:
        refs[-1][start : start + ref.shape[0], :] = ref[...]
        start += ref.shape[0]


def pack(*blocks):
    return pl.pallas_call(
        pack_kernel, out_shape=shape((512, 384)), name="pack", compiler_params=room(4)
    )(*blocks)


def beside_kernel(*refs):
    for k in range(3):
        refs[3][:, 384 * k : 384 * (k + 1)] = refs[k][...]


def beside(*blocks):
    return pl.pallas_call(
        beside_kernel, out_shape=shape((512, 1152)), name="beside", compiler_params=room(6)
    )(*blocks)


def halves_kernel(near_a, far_a, near_b, far_b, top, bottom):
    top[:, 0:1152] = near_a[0:256, :]
    top[:, 1152:1536] = far_a[0:256, :]
    bottom[:, 0:1152] = near_b[256:512, :]
    bottom[:, 1152:1536] = far_b[256:512, :]


def halves(*args):
    return pl.pallas_call(
        halves_kernel, out_shape=[shape((256, 1536))] * 2, name="halves", compiler_params=room(8)
    )(*args)


def act_first_kernel(table, *refs):
    pieces, down_own, down_other, acc = refs[:6], refs[6], refs[7], refs[8]
    for k, group in enumerate((0, 1, 3)):
        rows = jnp.concatenate([pieces[2 * k][...], pieces[2 * k + 1][...]], axis=1)
        for side, down in enumerate((down_own, down_other)):
            columns = [
                down[:, pl.ds(pl.multiple_of(table[4 * group + j] * 384, 384), 384)] for j in CHUNKS
            ]
            term = lax.dot_general(
                jnp.concatenate(columns, axis=1), rows, NT, preferred_element_type=F32
            )
            if k == 0:
                acc[256 * side : 256 * (side + 1), :] = term
            else:
                acc[256 * side : 256 * (side + 1), :] += term


def act_first(table, pieces, down_own, down_other):
    return pl.pallas_call(
        act_first_kernel,
        in_specs=[SM] + [VM] * 8,
        out_specs=VM,
        out_shape=shape((512, 512), F32),
        name="act_first",
        compiler_params=room(28),
    )(table, *pieces, down_own, down_other)


def act_last_kernel(table, *refs):
    rows = jnp.concatenate([refs[0][...], refs[1][...]], axis=0)
    acc, out = refs[10], refs[13]
    for side in range(2):
        columns = jnp.concatenate([refs[2 + 4 * side + j][...] for j in range(4)], axis=1)
        here = slice(256 * side, 256 * (side + 1))
        act = acc[here, :] + lax.dot_general(columns, rows, NT, preferred_element_type=F32)
        factor = refs[11 + side]
        out[256 * side : 256 * (side + 1), :] = (act * factor[0:256, :]).astype(BF)
        out[512 + 256 * side : 512 + 256 * (side + 1), :] = (act * factor[256:512, :]).astype(BF)


def act_last(table, pieces, down_own, down_other, acc, factor_own, factor_other):
    def column(j):
        return pl.BlockSpec((256, 384), lambda i, table: (0, table[8 + CHUNKS[j]]))

    def whole(dims):
        return pl.BlockSpec(dims, lambda i, table: (0, 0))

    columns = [column(j) for j in range(4)]
    return pl.pallas_call(
        act_last_kernel,
        grid_spec=pltpu.PrefetchScalarGridSpec(
            num_scalar_prefetch=1,
            grid=(1,),
            in_specs=[whole((256, 1536))] * 2 + columns * 2 + [whole((512, 512))] * 3,
            out_specs=whole((1024, 512)),
        ),
        out_shape=shape((1024, 512)),
        name="act_last",
        compiler_params=room(20),
    )(table, *pieces, *[down_own] * 4, *[down_other] * 4, acc, factor_own, factor_other)


def part_kernel(groups, per, table, *refs):
    weights, grads, outs = refs[: 4 * per], refs[4 * per], refs[4 * per + 1 :]
    step = pl.program_id(0)
    for j in range(per):
        weight = jnp.concatenate([weights[per * k + j][...] for k in range(4)], axis=1)
        total = lax.dot_general(weight, grads[...], NN, preferred_element_type=F32).astype(BF)
        for run, group in enumerate(groups):
            for piece in range(4 // per):
                chunk = per * piece + j

                @pl.when(step == 4 // per * run + piece)
                def _(total=total, run=run, group=group, chunk=chunk):
                    here = slice(384 * chunk, 384 * (chunk + 1))
                    if group == 2:
                        outs[0][here, :] = total[:, 0:256]
                        outs[1][here, :] = total[:, 256:512]
                    elif chunk == 3:
                        outs[2 * run + 1][...] = total
                    else:
                        outs[2 * run][here, :] = total


def part(table, grads, weights, groups, per):
    steps = 4 // per

    def rows(j):
        def index(i, table):
            place = per * (i % steps) + j
            chunk = jnp.where(place == 2, 3, jnp.where(place == 3, 2, place))
            group = groups[0] if len(groups) == 1 else jnp.where(i < steps, *groups)
            return (table[4 * group + chunk], 0)

        return pl.BlockSpec((384, 256), index)

    dims = []
    for group in groups:
        dims += [(1536, 256)] * 2 if group == 2 else [(1152, 512), (384, 512)]
    return pl.pallas_call(
        functools.partial(part_kernel, groups, per),
        grid_spec=pltpu.PrefetchScalarGridSpec(
            num_scalar_prefetch=1,
            grid=(steps * len(groups),),
            in_specs=[rows(j) for j in range(per)] * 4
            + [pl.BlockSpec((1024, 512), lambda i, table: (0, 0))],
            out_specs=[pl.BlockSpec(d, lambda i, table: (0, 0)) for d in dims],
        ),
        out_shape=[shape(d) for d in dims],
        compiler_params=room(20),
    )(table, *[w for weight in weights for w in [weight] * per], grads)


def add(*terms):
    total = terms[0].astype(F32)
    for term in terms[1:]:
        total = total + term.astype(F32)
    return total


def pairs_kernel(near_a, far_a, got_a, near_b, far_b, got_b, out_near_a, out_far_a, out_near_b, out_far_b):
    def some_rows(k, carry):
        here = pl.ds(pl.multiple_of(k * 128, 128), 128)
        out_near_a[here, 0:256] = add(near_a[here, 0:256], got_a[here, :]).astype(BF)
        out_near_a[here, 256:512] = near_a[here, 256:512]
        out_near_b[here, 0:256] = near_b[here, 0:256]
        out_near_b[here, 256:512] = add(near_b[here, 256:512], got_b[here, :]).astype(BF)
        return carry

    lax.fori_loop(0, 9, some_rows, 0)
    out_far_a[:, 0:256] = add(far_a[:, 0:256], got_a[1152:1536, :]).astype(BF)
    out_far_a[:, 256:512] = far_a[:, 256:512]
    out_far_b[:, 0:256] = far_b[:, 0:256]
    out_far_b[:, 256:512] = add(far_b[:, 256:512], got_b[1152:1536, :]).astype(BF)


def add_pairs(*args):
    return pl.pallas_call(
        pairs_kernel,
        out_shape=[shape((1152, 512)), shape((384, 512))] * 2,
        name="add_pairs",
        compiler_params=room(16),
    )(*args)


def far_kernel(own, got1, got2, out):
    out[...] = add(own[...], got1[...], got2[...]).astype(BF)


def middle_far(*args):
    return pl.pallas_call(
        far_kernel, out_shape=shape((384, 512)), name="middle_far", compiler_params=room(6)
    )(*args)


def near_kernel(mine, got1, got2, far, own, ahead, behind):
    for k, out in enumerate((own, ahead, behind)):

        def some_rows(r, carry, k=k, out=out):
            to = pl.ds(pl.multiple_of(r * 128, 128), 128)
            here = pl.ds(pl.multiple_of(384 * k + r * 128, 128), 128)
            total = add(mine[here, :], got1[here, :], got2[here, :])
            if k == 1:
                total = total + far[to, :].astype(F32)
            out[to, :] = total.astype(out.dtype)
            return carry

        lax.fori_loop(0, 3, some_rows, 0)


def middle_near(*args):
    return pl.pallas_call(
        near_kernel,
        out_shape=[shape((384, 512), F32), shape((384, 512)), shape((384, 512))],
        name="middle_near",
        compiler_params=room(16),
    )(*args)


def last_kernel(own, got1, got2, back1, back2, back3, near, across):
    rows = add(own[...], got1[...], got2[...]).T.astype(BF)
    back1[...] = rows[0:128]
    back2[...] = rows[128:256]
    back3[...] = rows[256:384]
    near[...] = rows[384:448]
    across[...] = rows[448:512]


def last(*args):
    return pl.pallas_call(
        last_kernel,
        out_shape=[shape((128, 384))] * 3 + [shape((64, 384))] * 2,
        name="last",
        compiler_params=room(8),
    )(*args)


def heads_kernel(tokens, weights, out):
    def some_rows(k, carry):
        here = pl.ds(pl.multiple_of(k * 256, 256), 256)
        out[here, :] = lax.dot_general(
            tokens[here, :], weights[...], NT, preferred_element_type=F32
        ).astype(BF)
        return carry

    lax.fori_loop(0, 2, some_rows, 0)


def heads(*args):
    return pl.pallas_call(
        heads_kernel, out_shape=shape((512, 1536)), name="heads", compiler_params=room(12)
    )(*args)


def body(d_out, expert_ids, gate_weights, saved_gate, saved_up, w_gate, w_up, w_down, w_out):
    expert = lax.axis_index("expert").astype(I32)
    etp = lax.axis_index("etp").astype(I32)
    tp = lax.axis_index("tp").astype(I32)
    y, x = etp // 4, etp % 4
    core = tp % 2
    z = 4 * (tp // 2) + expert
    direction = 1 - 2 * core

    i = jnp.arange(34, dtype=I32)
    d, j, q = i // 4, i % 4, i % 8
    feature = 4 * ((y + jnp.where(core == 0, d, j)) % 4) + (x + jnp.where(core == 0, j, d)) % 4
    holder = jnp.where(i < 24, core, 1 - core)
    step = jnp.where(q >= 6, 4 * (q - 6), (1 - 2 * holder) * (q // 2 + 1))
    place = (z - step + 16) % 8
    source_core = jnp.where((q < 6) & (q % 2 == 1), 1 - holder, holder)
    table = jnp.where(i < 16, feature, 4 * (place % 4) + 2 * (place // 4) + source_core)
    table = jnp.where(i == 32, expert, jnp.where(i == 33, direction, table))

    near, *mine, far, sel = dispatch(table, expert_ids.T, gate_weights.T, d_out)
    other = swap_core(far)
    across = shift_z(near, 4)
    received = []
    for k in (1, 2, 3):
        rows = jnp.concatenate([mine[k - 1], other[192 - 64 * k : 256 - 64 * k]])
        received.append(shift_z(rows, k))

    down_own, gate_own, up_own = w_down[0], w_gate[0], w_up[0]
    down_other = swap_core(down_own)
    gate_other = swap_core(gate_own)
    up_other = swap_core(up_own)
    factor_own, sent_factor = factors(table, saved_gate[0], saved_up[0])

    rows = pack(*received, near, across)
    ahead = shift_plane(rows, -1, True)
    behind = shift_plane(rows, 1, True)
    near, sent_factor = lax.optimization_barrier((beside(rows, ahead, behind), sent_factor))
    factor_other = swap_core(sent_factor)
    far = shift_plane(ahead, -1, True)

    behind_near = shift_plane(near, 1, False)
    ahead_near = shift_plane(near, -1, False)
    behind_far = shift_plane(far, 1, False)
    ahead_far = shift_plane(far, -1, False)
    top, bottom = halves(ahead_near, ahead_far, behind_near, behind_far)
    last_top = shift_plane(top, -1, False)
    last_bottom = shift_plane(bottom, 1, False)

    acc = act_first(
        table,
        (near, far, ahead_near, ahead_far, behind_near, behind_far),
        down_own,
        down_other,
    )
    grads = act_last(table, (last_top, last_bottom), down_own, down_other, acc, factor_own, factor_other)

    weights = (gate_own, gate_other, up_own, up_other)
    far_top, far_bottom = part(table, grads, weights, (2,), 2)
    got_top = shift_plane(far_top, 1, False)
    got_bottom = shift_plane(far_bottom, -1, False)
    ahead_near, ahead_far, behind_near, behind_far = part(table, grads, weights, (1, 3), 2)
    own_near, own_far = part(table, grads, weights, (0,), 1)
    up_near, up_far, down_near, down_far = add_pairs(
        ahead_near, ahead_far, got_top, behind_near, behind_far, got_bottom
    )
    from_behind_far = shift_plane(up_far, 1, False)
    from_ahead_far = shift_plane(down_far, -1, False)
    from_behind_near = shift_plane(up_near, 1, False)
    from_ahead_near = shift_plane(down_near, -1, False)

    got_far = shift_plane(middle_far(own_far, from_behind_far, from_ahead_far), 1, True)
    own, to_ahead, to_behind = middle_near(own_near, from_behind_near, from_ahead_near, got_far)
    from_behind = shift_plane(to_ahead, 1, True)
    from_ahead = shift_plane(to_behind, -1, True)
    *back, near, across = last(own, from_behind, from_ahead)

    across = shift_z(across, 4)
    returned = []
    for k, rows in zip((1, 2, 3), back):
        returned.append(shift_z(rows, -k))
    back = returned
    other = swap_core(jnp.concatenate([rows[64:128] for rows in back], axis=0))
    d_hidden = combine(sel, d_out, *back, other, near, across)

    head_partial = heads(lax.all_gather(d_hidden, "tp", axis=0, tiled=True), w_out)
    spread = lax.all_to_all(head_partial.reshape(16, 32, 1536), "etp", 0, 0, tiled=True)
    d_heads = jnp.sum(spread.astype(F32), axis=0).astype(BF)
    return (d_hidden, d_heads)


def solution(mesh):
    in_specs = (
        P(("expert", "tp"), "etp"),
        P(("expert", "tp"), None),
        P(("expert", "tp"), None),
        P("expert", None, ("etp", "tp")),
        P("expert", None, ("etp", "tp")),
        P("expert", None, ("etp", "tp")),
        P("expert", None, ("etp", "tp")),
        P("expert", ("etp", "tp"), None),
        P("tp", "etp"),
    )
    out_specs = (P(("expert", "tp"), "etp"), P(("expert", "etp"), "tp"))

    return jax.shard_map(body, mesh=mesh, in_specs=in_specs, out_specs=out_specs, check_vma=False)
```

```python
import functools

import jax
import jax.numpy as jnp
from jax import lax
from jax.experimental import pallas as pl
from jax.experimental.pallas import tpu as pltpu
from jax.sharding import PartitionSpec as P


BF = jnp.bfloat16
F32 = jnp.float32
I32 = jnp.int32

NN = (((1,), (0,)), ((), ()))
NT = (((1,), (1,)), ((), ()))
VM = pl.BlockSpec(memory_space=pltpu.VMEM)
SM = pl.BlockSpec(memory_space=pltpu.SMEM)


CHUNKS = (0, 1, 3, 2)


def room(mib):
    return pltpu.CompilerParams(vmem_limit_bytes=mib << 20)


def shape(dims, kind=BF):
    return jax.ShapeDtypeStruct(dims, kind)


def shift_plane(value, step, first):
    pairs = []
    for y in range(4):
        for x in range(4):
            for t in range(4):
                along_x = (t % 2 == 0) == first
                to_y = y if along_x else (y + step) % 4
                to_x = (x + step) % 4 if along_x else x
                pairs.append((16 * y + 4 * x + t, 16 * to_y + 4 * to_x + t))
    return lax.ppermute(value, ("etp", "tp"), pairs)


def shift_z(value, step):
    pairs = []
    for low in range(4):
        for high in range(2):
            for core in range(2):
                to = (4 * high + low + (step if core == 0 else -step)) % 8
                pairs.append((4 * low + 2 * high + core, 4 * (to % 4) + 2 * (to // 4) + core))
    return lax.ppermute(value, ("expert", "tp"), pairs)


def swap_core(value):
    return lax.ppermute(value, "tp", [(t, t ^ 1) for t in range(4)])


def dispatch_kernel(table, ids, gates, grads, near, far, sel_out):
    expert = (table[32] + table[33] * lax.broadcasted_iota(I32, (8, 128), 0)) & 3
    hit0 = ids[0:1, :] == expert
    hit1 = ids[1:2, :] == expert
    zero = jnp.zeros((8, 128), F32)
    member = jnp.where(hit0 | hit1, 1.0, zero)
    weight = jnp.where(hit0, gates[0:1, :], zero) + jnp.where(hit1, gates[1:2, :], zero)
    before = lax.broadcasted_iota(I32, (128, 128), 0) < lax.broadcasted_iota(I32, (128, 128), 1)
    before = jnp.where(before, 1.0, jnp.zeros((128, 128), F32)).astype(BF)
    slot = jnp.dot(member.astype(BF), before, preferred_element_type=F32)
    slot_iota = lax.broadcasted_iota(I32, (64, 128), 0).astype(F32)
    for s in range(4):
        sel = jnp.where(slot[s : s + 1, :] == slot_iota, member[s : s + 1, :], 0.0)
        sel_bf = sel.astype(BF)
        rows = jnp.dot(sel_bf, grads[...], preferred_element_type=F32)
        row_weight = jnp.sum(sel * weight[s : s + 1, :], axis=1, keepdims=True)
        rows = (rows * row_weight).astype(BF)
        if s == 0:
            near[...] = rows
        else:
            far[64 * (s - 1) : 64 * s, :] = rows
        sel_out[64 * s : 64 * (s + 1), :] = sel_bf


def dispatch(table, ids, gates, grads):
    return pl.pallas_call(
        dispatch_kernel,
        in_specs=[SM, VM, VM, VM],
        out_specs=[VM] * 3,
        out_shape=[shape((64, 384)), shape((192, 384)), shape((256, 128))],
        name="dispatch",
    )(table, ids, gates, grads)


def messages_kernel(far, other, own, out1, out2, out3, near):
    for k, out in enumerate((out1, out2, out3)):
        out[0:64, :] = far[64 * k : 64 * (k + 1), :]
        out[64:128, :] = other[64 * (2 - k) : 64 * (3 - k), :]
    near[...] = own[...]


def messages(*args):
    return pl.pallas_call(
        messages_kernel,
        out_shape=[shape((128, 384))] * 3 + [shape((64, 384))],
        name="messages",
        compiler_params=room(4),
    )(*args)


def combine_kernel(sel, grads, from1, from2, from3, other, own, across, out):
    rows = jnp.concatenate(
        [from1[0:64], from2[0:64], from3[0:64], other[...], own[...], across[...]], axis=0
    )
    order = (1, 2, 3, 3, 2, 1, 0, 0)
    picks = jnp.concatenate([sel[64 * k : 64 * (k + 1)] for k in order], axis=0)
    moe = lax.dot_general(picks, rows, (((0,), (0,)), ((), ())), preferred_element_type=F32)
    out[...] = (grads[...].astype(F32) + moe).astype(BF)


def combine(*args):
    return pl.pallas_call(
        combine_kernel, out_shape=shape((128, 384)), name="combine", compiler_params=room(4)
    )(*args)


def factors_kernel(table, gates, ups, mine, theirs, to_gate, to_up):
    for side, out in enumerate((mine, theirs)):

        def block_step(block, carry, side=side):
            start = pl.multiple_of(table[16 + 8 * side + block] * 64, 64)
            here = pl.ds(pl.multiple_of(block * 64, 64), 64)
            gate = gates[pl.ds(start, 64), :].astype(F32)
            up = ups[pl.ds(start, 64), :].astype(F32)
            sigma = 1.0 / (1.0 + jnp.exp(-gate))
            to_gate[here, :] = up * sigma * (1.0 + gate * (1.0 - sigma))
            to_up[here, :] = gate * sigma
            return carry

        lax.fori_loop(0, 8, block_step, 0)
        out[0:256, :] = to_gate[...].T
        out[256:512, :] = to_up[...].T


def factors(table, *saved):
    return pl.pallas_call(
        factors_kernel,
        in_specs=[SM] + [VM] * 2,
        out_specs=[VM] * 2,
        out_shape=[shape((512, 512), F32)] * 2,
        scratch_shapes=[pltpu.VMEM((512, 256), F32)] * 2,
        name="factors",
        compiler_params=room(16),
    )(table, *saved)


def pack_kernel(*refs):
    start = 0
    for ref in refs[:-1]:
        refs[-1][start : start + ref.shape[0], :] = ref[...]
        start += ref.shape[0]


def pack(*blocks):
    return pl.pallas_call(
        pack_kernel, out_shape=shape((512, 384)), name="pack", compiler_params=room(4)
    )(*blocks)


def beside_kernel(*refs):
    for k in range(3):
        refs[3][:, 384 * k : 384 * (k + 1)] = refs[k][...]


def beside(*blocks):
    return pl.pallas_call(
        beside_kernel, out_shape=shape((512, 1152)), name="beside", compiler_params=room(6)
    )(*blocks)


def halves_kernel(near_a, far_a, near_b, far_b, top, bottom):
    top[:, 0:1152] = near_a[0:256, :]
    top[:, 1152:1536] = far_a[0:256, :]
    bottom[:, 0:1152] = near_b[256:512, :]
    bottom[:, 1152:1536] = far_b[256:512, :]


def halves(*args):
    return pl.pallas_call(
        halves_kernel, out_shape=[shape((256, 1536))] * 2, name="halves", compiler_params=room(8)
    )(*args)


def act_first_kernel(table, *refs):
    pieces, down_own, down_other, acc = refs[:6], refs[6], refs[7], refs[8]
    for k, group in enumerate((0, 1, 3)):
        rows = jnp.concatenate([pieces[2 * k][...], pieces[2 * k + 1][...]], axis=1)
        for side, down in enumerate((down_own, down_other)):
            columns = [
                down[:, pl.ds(pl.multiple_of(table[4 * group + j] * 384, 384), 384)] for j in CHUNKS
            ]
            term = lax.dot_general(
                jnp.concatenate(columns, axis=1), rows, NT, preferred_element_type=F32
            )
            if k == 0:
                acc[256 * side : 256 * (side + 1), :] = term
            else:
                acc[256 * side : 256 * (side + 1), :] += term


def act_first(table, pieces, down_own, down_other):
    return pl.pallas_call(
        act_first_kernel,
        in_specs=[SM] + [VM] * 8,
        out_specs=VM,
        out_shape=shape((512, 512), F32),
        name="act_first",
        compiler_params=room(28),
    )(table, *pieces, down_own, down_other)


def act_last_kernel(table, *refs):
    rows = jnp.concatenate([refs[0][...], refs[1][...]], axis=0)
    acc, out = refs[10], refs[13]
    for side in range(2):
        columns = jnp.concatenate([refs[2 + 4 * side + j][...] for j in range(4)], axis=1)
        here = slice(256 * side, 256 * (side + 1))
        act = acc[here, :] + lax.dot_general(columns, rows, NT, preferred_element_type=F32)
        factor = refs[11 + side]
        out[256 * side : 256 * (side + 1), :] = (act * factor[0:256, :]).astype(BF)
        out[512 + 256 * side : 512 + 256 * (side + 1), :] = (act * factor[256:512, :]).astype(BF)


def act_last(table, pieces, down_own, down_other, acc, factor_own, factor_other):
    def column(j):
        return pl.BlockSpec((256, 384), lambda i, table: (0, table[8 + CHUNKS[j]]))

    def whole(dims):
        return pl.BlockSpec(dims, lambda i, table: (0, 0))

    columns = [column(j) for j in range(4)]
    return pl.pallas_call(
        act_last_kernel,
        grid_spec=pltpu.PrefetchScalarGridSpec(
            num_scalar_prefetch=1,
            grid=(1,),
            in_specs=[whole((256, 1536))] * 2 + columns * 2 + [whole((512, 512))] * 3,
            out_specs=whole((1024, 512)),
        ),
        out_shape=shape((1024, 512)),
        name="act_last",
        compiler_params=room(20),
    )(table, *pieces, *[down_own] * 4, *[down_other] * 4, acc, factor_own, factor_other)


def part_kernel(groups, per, table, *refs):
    weights, grads, outs = refs[: 4 * per], refs[4 * per], refs[4 * per + 1 :]
    step = pl.program_id(0)
    for j in range(per):
        weight = jnp.concatenate([weights[per * k + j][...] for k in range(4)], axis=1)
        total = lax.dot_general(weight, grads[...], NN, preferred_element_type=F32).astype(BF)
        for run, group in enumerate(groups):
            for piece in range(4 // per):
                chunk = per * piece + j

                @pl.when(step == 4 // per * run + piece)
                def _(total=total, run=run, group=group, chunk=chunk):
                    here = slice(384 * chunk, 384 * (chunk + 1))
                    if group == 2:
                        outs[0][here, :] = total[:, 0:256]
                        outs[1][here, :] = total[:, 256:512]
                    elif chunk == 3:
                        outs[2 * run + 1][...] = total
                    else:
                        outs[2 * run][here, :] = total


def part(table, grads, weights, groups, per):
    steps = 4 // per

    def rows(j):
        def index(i, table):
            place = per * (i % steps) + j
            chunk = jnp.where(place == 2, 3, jnp.where(place == 3, 2, place))
            group = groups[0] if len(groups) == 1 else jnp.where(i < steps, *groups)
            return (table[4 * group + chunk], 0)

        return pl.BlockSpec((384, 256), index)

    dims = []
    for group in groups:
        dims += [(1536, 256)] * 2 if group == 2 else [(1152, 512), (384, 512)]
    return pl.pallas_call(
        functools.partial(part_kernel, groups, per),
        grid_spec=pltpu.PrefetchScalarGridSpec(
            num_scalar_prefetch=1,
            grid=(steps * len(groups),),
            in_specs=[rows(j) for j in range(per)] * 4
            + [pl.BlockSpec((1024, 512), lambda i, table: (0, 0))],
            out_specs=[pl.BlockSpec(d, lambda i, table: (0, 0)) for d in dims],
        ),
        out_shape=[shape(d) for d in dims],
        compiler_params=room(20),
    )(table, *[w for weight in weights for w in [weight] * per], grads)


def add(*terms):
    total = terms[0].astype(F32)
    for term in terms[1:]:
        total = total + term.astype(F32)
    return total


def pairs_kernel(near_a, far_a, got_a, near_b, far_b, got_b, out_near_a, out_far_a, out_near_b, out_far_b):
    def some_rows(k, carry):
        here = pl.ds(pl.multiple_of(k * 128, 128), 128)
        out_near_a[here, 0:256] = add(near_a[here, 0:256], got_a[here, :]).astype(BF)
        out_near_a[here, 256:512] = near_a[here, 256:512]
        out_near_b[here, 0:256] = near_b[here, 0:256]
        out_near_b[here, 256:512] = add(near_b[here, 256:512], got_b[here, :]).astype(BF)
        return carry

    lax.fori_loop(0, 9, some_rows, 0)
    out_far_a[:, 0:256] = add(far_a[:, 0:256], got_a[1152:1536, :]).astype(BF)
    out_far_a[:, 256:512] = far_a[:, 256:512]
    out_far_b[:, 0:256] = far_b[:, 0:256]
    out_far_b[:, 256:512] = add(far_b[:, 256:512], got_b[1152:1536, :]).astype(BF)


def add_pairs(*args):
    return pl.pallas_call(
        pairs_kernel,
        out_shape=[shape((1152, 512)), shape((384, 512))] * 2,
        name="add_pairs",
        compiler_params=room(16),
    )(*args)


def far_kernel(own, got1, got2, top, bottom):
    total = add(own[...], got1[...], got2[...]).astype(BF)
    top[...] = total[:, 0:256]
    bottom[...] = total[:, 256:512]


def middle_far(*args):
    return pl.pallas_call(
        far_kernel, out_shape=[shape((384, 256))] * 2, name="middle_far", compiler_params=room(6)
    )(*args)


def near_kernel(mine, got1, got2, far_top, far_bottom, own, ahead, behind):
    for k, out in enumerate((own, ahead, behind)):

        def some_rows(r, carry, k=k, out=out):
            to = pl.ds(pl.multiple_of(r * 128, 128), 128)
            here = pl.ds(pl.multiple_of(384 * k + r * 128, 128), 128)
            total = add(mine[here, :], got1[here, :], got2[here, :])
            top, bottom = total[:, 0:256], total[:, 256:512]
            if k == 1:
                top = top + far_top[to, :].astype(F32)
            if k == 2:
                bottom = bottom + far_bottom[to, :].astype(F32)
            out[to, 0:256] = top.astype(out.dtype)
            out[to, 256:512] = bottom.astype(out.dtype)
            return carry

        lax.fori_loop(0, 3, some_rows, 0)


def middle_near(*args):
    return pl.pallas_call(
        near_kernel,
        out_shape=[shape((384, 512), F32), shape((384, 512)), shape((384, 512))],
        name="middle_near",
        compiler_params=room(16),
    )(*args)


def last_kernel(own, got1, got2, back1, back2, back3, near, across):
    rows = add(own[...], got1[...], got2[...]).T.astype(BF)
    back1[...] = rows[0:128]
    back2[...] = rows[128:256]
    back3[...] = rows[256:384]
    near[...] = rows[384:448]
    across[...] = rows[448:512]


def last(*args):
    return pl.pallas_call(
        last_kernel,
        out_shape=[shape((128, 384))] * 3 + [shape((64, 384))] * 2,
        name="last",
        compiler_params=room(8),
    )(*args)


def heads_kernel(tokens, weights, out):
    def some_rows(k, carry):
        here = pl.ds(pl.multiple_of(k * 256, 256), 256)
        out[here, :] = lax.dot_general(
            tokens[here, :], weights[...], NT, preferred_element_type=F32
        ).astype(BF)
        return carry

    lax.fori_loop(0, 2, some_rows, 0)


def heads(*args):
    return pl.pallas_call(
        heads_kernel, out_shape=shape((512, 1536)), name="heads", compiler_params=room(12)
    )(*args)


def body(d_out, expert_ids, gate_weights, saved_gate, saved_up, w_gate, w_up, w_down, w_out):
    expert = lax.axis_index("expert").astype(I32)
    etp = lax.axis_index("etp").astype(I32)
    tp = lax.axis_index("tp").astype(I32)
    y, x = etp // 4, etp % 4
    core = tp % 2
    z = 4 * (tp // 2) + expert
    direction = 1 - 2 * core

    i = jnp.arange(34, dtype=I32)
    d, j, q = i // 4, i % 4, i % 8
    feature = 4 * ((y + jnp.where(core == 0, d, j)) % 4) + (x + jnp.where(core == 0, j, d)) % 4
    holder = jnp.where(i < 24, core, 1 - core)
    step = jnp.where(q >= 6, 4 * (q - 6), (1 - 2 * holder) * (q // 2 + 1))
    place = (z - step + 16) % 8
    source_core = jnp.where((q < 6) & (q % 2 == 1), 1 - holder, holder)
    table = jnp.where(i < 16, feature, 4 * (place % 4) + 2 * (place // 4) + source_core)
    table = jnp.where(i == 32, expert, jnp.where(i == 33, direction, table))

    near, far, sel = dispatch(table, expert_ids.T, gate_weights.T, d_out)
    other = swap_core(far)
    across = shift_z(near, 4)
    *sent, near = messages(far, other, near)
    received = []
    for k, rows in zip((1, 2, 3), sent):
        received.append(shift_z(rows, k))

    down_own, gate_own, up_own = w_down[0], w_gate[0], w_up[0]
    down_other = swap_core(down_own)
    gate_other = swap_core(gate_own)
    up_other = swap_core(up_own)
    factor_own, sent_factor = factors(table, saved_gate[0], saved_up[0])

    rows = pack(*received, near, across)
    ahead = shift_plane(rows, -1, True)
    behind = shift_plane(rows, 1, True)
    near, sent_factor = lax.optimization_barrier((beside(rows, ahead, behind), sent_factor))
    factor_other = swap_core(sent_factor)
    far_top = shift_plane(ahead[:256], -1, True)
    far_bottom = shift_plane(behind[256:], 1, True)
    far = jnp.concatenate([far_top, far_bottom], axis=0)

    behind_near = shift_plane(near, 1, False)
    ahead_near = shift_plane(near, -1, False)
    behind_far = shift_plane(far, 1, False)
    ahead_far = shift_plane(far, -1, False)
    top, bottom = halves(ahead_near, ahead_far, behind_near, behind_far)
    last_top = shift_plane(top, -1, False)
    last_bottom = shift_plane(bottom, 1, False)

    acc = act_first(
        table,
        (near, far, ahead_near, ahead_far, behind_near, behind_far),
        down_own,
        down_other,
    )
    grads = act_last(table, (last_top, last_bottom), down_own, down_other, acc, factor_own, factor_other)

    weights = (gate_own, gate_other, up_own, up_other)
    far_top, far_bottom = part(table, grads, weights, (2,), 2)
    got_top = shift_plane(far_top, 1, False)
    got_bottom = shift_plane(far_bottom, -1, False)
    ahead_near, ahead_far, behind_near, behind_far = part(table, grads, weights, (1, 3), 2)
    own_near, own_far = part(table, grads, weights, (0,), 1)
    up_near, up_far, down_near, down_far = add_pairs(
        ahead_near, ahead_far, got_top, behind_near, behind_far, got_bottom
    )
    from_behind_far = shift_plane(up_far, 1, False)
    from_ahead_far = shift_plane(down_far, -1, False)
    from_behind_near = shift_plane(up_near, 1, False)
    from_ahead_near = shift_plane(down_near, -1, False)

    far_top, far_bottom = middle_far(own_far, from_behind_far, from_ahead_far)
    got_top = shift_plane(far_top, 1, True)
    got_bottom = shift_plane(far_bottom, -1, True)
    own, to_ahead, to_behind = middle_near(
        own_near, from_behind_near, from_ahead_near, got_top, got_bottom
    )
    from_behind = shift_plane(to_ahead, 1, True)
    from_ahead = shift_plane(to_behind, -1, True)
    *back, near, across = last(own, from_behind, from_ahead)

    across = shift_z(across, 4)
    returned = []
    for k, rows in zip((1, 2, 3), back):
        returned.append(shift_z(rows, -k))
    back = returned
    other = swap_core(jnp.concatenate([rows[64:128] for rows in back], axis=0))
    d_hidden = combine(sel, d_out, *back, other, near, across)

    head_partial = heads(lax.all_gather(d_hidden, "tp", axis=0, tiled=True), w_out)
    spread = lax.all_to_all(head_partial.reshape(16, 32, 1536), "etp", 0, 0, tiled=True)
    d_heads = jnp.sum(spread.astype(F32), axis=0).astype(BF)
    return (d_hidden, d_heads)


def solution(mesh):
    in_specs = (
        P(("expert", "tp"), "etp"),
        P(("expert", "tp"), None),
        P(("expert", "tp"), None),
        P("expert", None, ("etp", "tp")),
        P("expert", None, ("etp", "tp")),
        P("expert", None, ("etp", "tp")),
        P("expert", None, ("etp", "tp")),
        P("expert", ("etp", "tp"), None),
        P("tp", "etp"),
    )
    out_specs = (P(("expert", "tp"), "etp"), P(("expert", "etp"), "tp"))

    return jax.shard_map(body, mesh=mesh, in_specs=in_specs, out_specs=out_specs, check_vma=False)
```

```python
import functools

import jax
import jax.numpy as jnp
from jax import lax
from jax.experimental import pallas as pl
from jax.experimental.pallas import tpu as pltpu
from jax.sharding import PartitionSpec as P


BF = jnp.bfloat16
F32 = jnp.float32
I32 = jnp.int32

NN = (((1,), (0,)), ((), ()))
NT = (((1,), (1,)), ((), ()))
VM = pl.BlockSpec(memory_space=pltpu.VMEM)
SM = pl.BlockSpec(memory_space=pltpu.SMEM)


CHUNKS = (0, 1, 3, 2)


def room(mib):
    return pltpu.CompilerParams(vmem_limit_bytes=mib << 20)


def shape(dims, kind=BF):
    return jax.ShapeDtypeStruct(dims, kind)


def shift_plane(value, step, first):
    pairs = []
    for y in range(4):
        for x in range(4):
            for t in range(4):
                along_x = (t % 2 == 0) == first
                to_y = y if along_x else (y + step) % 4
                to_x = (x + step) % 4 if along_x else x
                pairs.append((16 * y + 4 * x + t, 16 * to_y + 4 * to_x + t))
    return lax.ppermute(value, ("etp", "tp"), pairs)


def shift_z(value, step):
    pairs = []
    for low in range(4):
        for high in range(2):
            for core in range(2):
                to = (4 * high + low + (step if core == 0 else -step)) % 8
                pairs.append((4 * low + 2 * high + core, 4 * (to % 4) + 2 * (to // 4) + core))
    return lax.ppermute(value, ("expert", "tp"), pairs)


def swap_core(value):
    return lax.ppermute(value, "tp", [(t, t ^ 1) for t in range(4)])


def dispatch_kernel(table, ids, gates, grads, near, far, sel_out):
    expert = (table[32] + table[33] * lax.broadcasted_iota(I32, (8, 128), 0)) & 3
    hit0 = ids[0:1, :] == expert
    hit1 = ids[1:2, :] == expert
    zero = jnp.zeros((8, 128), F32)
    member = jnp.where(hit0 | hit1, 1.0, zero)
    weight = jnp.where(hit0, gates[0:1, :], zero) + jnp.where(hit1, gates[1:2, :], zero)
    before = lax.broadcasted_iota(I32, (128, 128), 0) < lax.broadcasted_iota(I32, (128, 128), 1)
    before = jnp.where(before, 1.0, jnp.zeros((128, 128), F32)).astype(BF)
    slot = jnp.dot(member.astype(BF), before, preferred_element_type=F32)
    slot_iota = lax.broadcasted_iota(I32, (64, 128), 0).astype(F32)
    for s in range(4):
        sel = jnp.where(slot[s : s + 1, :] == slot_iota, member[s : s + 1, :], 0.0)
        sel_bf = sel.astype(BF)
        rows = jnp.dot(sel_bf, grads[...], preferred_element_type=F32)
        row_weight = jnp.sum(sel * weight[s : s + 1, :], axis=1, keepdims=True)
        rows = (rows * row_weight).astype(BF)
        if s == 0:
            near[...] = rows
        else:
            far[64 * (s - 1) : 64 * s, :] = rows
        sel_out[64 * s : 64 * (s + 1), :] = sel_bf


def dispatch(table, ids, gates, grads):
    return pl.pallas_call(
        dispatch_kernel,
        in_specs=[SM, VM, VM, VM],
        out_specs=[VM] * 3,
        out_shape=[shape((64, 384)), shape((192, 384)), shape((256, 128))],
        name="dispatch",
    )(table, ids, gates, grads)


def messages_kernel(far, other, own, out1, out2, out3, near):
    for k, out in enumerate((out1, out2, out3)):
        out[0:64, :] = far[64 * k : 64 * (k + 1), :]
        out[64:128, :] = other[64 * (2 - k) : 64 * (3 - k), :]
    near[...] = own[...]


def messages(*args):
    return pl.pallas_call(
        messages_kernel,
        out_shape=[shape((128, 384))] * 3 + [shape((64, 384))],
        name="messages",
        compiler_params=room(4),
    )(*args)


def combine_kernel(sel, grads, from1, from2, from3, other, own, across, out):
    rows = jnp.concatenate(
        [from1[0:64], from2[0:64], from3[0:64], other[...], own[...], across[...]], axis=0
    )
    order = (1, 2, 3, 3, 2, 1, 0, 0)
    picks = jnp.concatenate([sel[64 * k : 64 * (k + 1)] for k in order], axis=0)
    moe = lax.dot_general(picks, rows, (((0,), (0,)), ((), ())), preferred_element_type=F32)
    out[...] = (grads[...].astype(F32) + moe).astype(BF)


def combine(*args):
    return pl.pallas_call(
        combine_kernel, out_shape=shape((128, 384)), name="combine", compiler_params=room(4)
    )(*args)


def factors_kernel(table, gates, ups, mine, theirs, to_gate, to_up):
    for side, out in enumerate((mine, theirs)):

        def block_step(block, carry, side=side):
            start = pl.multiple_of(table[16 + 8 * side + block] * 64, 64)
            here = pl.ds(pl.multiple_of(block * 64, 64), 64)
            gate = gates[pl.ds(start, 64), :].astype(F32)
            up = ups[pl.ds(start, 64), :].astype(F32)
            sigma = 1.0 / (1.0 + jnp.exp(-gate))
            to_gate[here, :] = up * sigma * (1.0 + gate * (1.0 - sigma))
            to_up[here, :] = gate * sigma
            return carry

        lax.fori_loop(0, 8, block_step, 0)
        out[0:256, :] = to_gate[...].T
        out[256:512, :] = to_up[...].T


def factors(table, *saved):
    return pl.pallas_call(
        factors_kernel,
        in_specs=[SM] + [VM] * 2,
        out_specs=[VM] * 2,
        out_shape=[shape((512, 512), F32)] * 2,
        scratch_shapes=[pltpu.VMEM((512, 256), F32)] * 2,
        name="factors",
        compiler_params=room(16),
    )(table, *saved)


def pack_kernel(*refs):
    start = 0
    for ref in refs[:-1]:
        refs[-1][start : start + ref.shape[0], :] = ref[...]
        start += ref.shape[0]


def pack(*blocks):
    return pl.pallas_call(
        pack_kernel, out_shape=shape((512, 384)), name="pack", compiler_params=room(4)
    )(*blocks)


def beside_kernel(own, ahead, behind, top, bottom):
    for k, ref in enumerate((own, ahead, behind)):
        top[:, 384 * k : 384 * (k + 1)] = ref[0:256, :]
        bottom[:, 384 * k : 384 * (k + 1)] = ref[256:512, :]


def beside(*blocks):
    return pl.pallas_call(
        beside_kernel, out_shape=[shape((256, 1152))] * 2, name="beside", compiler_params=room(6)
    )(*blocks)


def halves_kernel(near_a, far_a, near_b, far_b, top, bottom):
    top[:, 0:1152] = near_a[...]
    top[:, 1152:1536] = far_a[0:256, :]
    bottom[:, 0:1152] = near_b[...]
    bottom[:, 1152:1536] = far_b[256:512, :]


def halves(*args):
    return pl.pallas_call(
        halves_kernel, out_shape=[shape((256, 1536))] * 2, name="halves", compiler_params=room(8)
    )(*args)


def act_first_kernel(table, *refs):
    pieces, down_own, down_other, acc = refs[:9], refs[9], refs[10], refs[11]
    for k, group in enumerate((0, 1, 3)):
        top, bottom, far = pieces[3 * k : 3 * k + 3]
        rows = jnp.concatenate(
            [jnp.concatenate([top[...], bottom[...]], axis=0), far[...]], axis=1
        )
        for side, down in enumerate((down_own, down_other)):
            columns = [
                down[:, pl.ds(pl.multiple_of(table[4 * group + j] * 384, 384), 384)] for j in CHUNKS
            ]
            term = lax.dot_general(
                jnp.concatenate(columns, axis=1), rows, NT, preferred_element_type=F32
            )
            if k == 0:
                acc[256 * side : 256 * (side + 1), :] = term
            else:
                acc[256 * side : 256 * (side + 1), :] += term


def act_first(table, pieces, down_own, down_other):
    return pl.pallas_call(
        act_first_kernel,
        in_specs=[SM] + [VM] * 11,
        out_specs=VM,
        out_shape=shape((512, 512), F32),
        name="act_first",
        compiler_params=room(28),
    )(table, *pieces, down_own, down_other)


def act_last_kernel(table, *refs):
    rows = jnp.concatenate([refs[0][...], refs[1][...]], axis=0)
    acc, out = refs[10], refs[13]
    for side in range(2):
        columns = jnp.concatenate([refs[2 + 4 * side + j][...] for j in range(4)], axis=1)
        here = slice(256 * side, 256 * (side + 1))
        act = acc[here, :] + lax.dot_general(columns, rows, NT, preferred_element_type=F32)
        factor = refs[11 + side]
        out[256 * side : 256 * (side + 1), :] = (act * factor[0:256, :]).astype(BF)
        out[512 + 256 * side : 512 + 256 * (side + 1), :] = (act * factor[256:512, :]).astype(BF)


def act_last(table, pieces, down_own, down_other, acc, factor_own, factor_other):
    def column(j):
        return pl.BlockSpec((256, 384), lambda i, table: (0, table[8 + CHUNKS[j]]))

    def whole(dims):
        return pl.BlockSpec(dims, lambda i, table: (0, 0))

    columns = [column(j) for j in range(4)]
    return pl.pallas_call(
        act_last_kernel,
        grid_spec=pltpu.PrefetchScalarGridSpec(
            num_scalar_prefetch=1,
            grid=(1,),
            in_specs=[whole((256, 1536))] * 2 + columns * 2 + [whole((512, 512))] * 3,
            out_specs=whole((1024, 512)),
        ),
        out_shape=shape((1024, 512)),
        name="act_last",
        compiler_params=room(20),
    )(table, *pieces, *[down_own] * 4, *[down_other] * 4, acc, factor_own, factor_other)


def part_kernel(groups, per, table, *refs):
    weights, grads, outs = refs[: 4 * per], refs[4 * per], refs[4 * per + 1 :]
    step = pl.program_id(0)
    for j in range(per):
        weight = jnp.concatenate([weights[per * k + j][...] for k in range(4)], axis=1)
        total = lax.dot_general(weight, grads[...], NN, preferred_element_type=F32).astype(BF)
        for run, group in enumerate(groups):
            for piece in range(4 // per):
                chunk = per * piece + j

                @pl.when(step == 4 // per * run + piece)
                def _(total=total, run=run, group=group, chunk=chunk):
                    here = slice(384 * chunk, 384 * (chunk + 1))
                    if group == 0 and chunk == 3:
                        outs[1][...] = total
                    elif group == 0:
                        outs[0][here, :] = total
                    elif group != 2 and chunk == 3:
                        outs[3 * run + 2][...] = total
                    else:
                        outs[3 * run][here, :] = total[:, 0:256]
                        outs[3 * run + 1][here, :] = total[:, 256:512]


def part(table, grads, weights, groups, per):
    steps = 4 // per

    def rows(j):
        def index(i, table):
            place = per * (i % steps) + j
            chunk = jnp.where(place == 2, 3, jnp.where(place == 3, 2, place))
            group = groups[0] if len(groups) == 1 else jnp.where(i < steps, *groups)
            return (table[4 * group + chunk], 0)

        return pl.BlockSpec((384, 256), index)

    dims = []
    for group in groups:
        if group == 2:
            dims += [(1536, 256)] * 2
        elif group == 0:
            dims += [(1152, 512), (384, 512)]
        else:
            dims += [(1152, 256), (1152, 256), (384, 512)]
    return pl.pallas_call(
        functools.partial(part_kernel, groups, per),
        grid_spec=pltpu.PrefetchScalarGridSpec(
            num_scalar_prefetch=1,
            grid=(steps * len(groups),),
            in_specs=[rows(j) for j in range(per)] * 4
            + [pl.BlockSpec((1024, 512), lambda i, table: (0, 0))],
            out_specs=[pl.BlockSpec(d, lambda i, table: (0, 0)) for d in dims],
        ),
        out_shape=[shape(d) for d in dims],
        compiler_params=room(20),
    )(table, *[w for weight in weights for w in [weight] * per], grads)


def add(*terms):
    total = terms[0].astype(F32)
    for term in terms[1:]:
        total = total + term.astype(F32)
    return total


def pairs_kernel(near_a, far_a, got_a, near_b, far_b, got_b, out_near_a, out_far_a, out_near_b, out_far_b):
    def some_rows(k, carry):
        here = pl.ds(pl.multiple_of(k * 128, 128), 128)
        out_near_a[here, :] = add(near_a[here, :], got_a[here, :]).astype(BF)
        out_near_b[here, :] = add(near_b[here, :], got_b[here, :]).astype(BF)
        return carry

    lax.fori_loop(0, 9, some_rows, 0)
    out_far_a[:, 0:256] = add(far_a[:, 0:256], got_a[1152:1536, :]).astype(BF)
    out_far_a[:, 256:512] = far_a[:, 256:512]
    out_far_b[:, 0:256] = far_b[:, 0:256]
    out_far_b[:, 256:512] = add(far_b[:, 256:512], got_b[1152:1536, :]).astype(BF)


def add_pairs(*args):
    return pl.pallas_call(
        pairs_kernel,
        out_shape=[shape((1152, 256)), shape((384, 512))] * 2,
        name="add_pairs",
        compiler_params=room(16),
    )(*args)


def far_kernel(own, got1, got2, top, bottom):
    total = add(own[...], got1[...], got2[...]).astype(BF)
    top[...] = total[:, 0:256]
    bottom[...] = total[:, 256:512]


def middle_far(*args):
    return pl.pallas_call(
        far_kernel, out_shape=[shape((384, 256))] * 2, name="middle_far", compiler_params=room(6)
    )(*args)


def near_kernel(mine, top1, top2, bottom1, bottom2, far_top, far_bottom, own, ahead, behind):
    for k, out in enumerate((own, ahead, behind)):

        def some_rows(r, carry, k=k, out=out):
            to = pl.ds(pl.multiple_of(r * 128, 128), 128)
            here = pl.ds(pl.multiple_of(384 * k + r * 128, 128), 128)
            top = add(mine[here, 0:256], top1[here, :], top2[here, :])
            bottom = add(mine[here, 256:512], bottom1[here, :], bottom2[here, :])
            if k == 1:
                top = top + far_top[to, :].astype(F32)
            if k == 2:
                bottom = bottom + far_bottom[to, :].astype(F32)
            out[to, 0:256] = top.astype(out.dtype)
            out[to, 256:512] = bottom.astype(out.dtype)
            return carry

        lax.fori_loop(0, 3, some_rows, 0)


def middle_near(*args):
    return pl.pallas_call(
        near_kernel,
        out_shape=[shape((384, 512), F32), shape((384, 512)), shape((384, 512))],
        name="middle_near",
        compiler_params=room(16),
    )(*args)


def last_kernel(own, got1, got2, back1, back2, back3, near, across):
    rows = add(own[...], got1[...], got2[...]).T.astype(BF)
    back1[...] = rows[0:128]
    back2[...] = rows[128:256]
    back3[...] = rows[256:384]
    near[...] = rows[384:448]
    across[...] = rows[448:512]


def last(*args):
    return pl.pallas_call(
        last_kernel,
        out_shape=[shape((128, 384))] * 3 + [shape((64, 384))] * 2,
        name="last",
        compiler_params=room(8),
    )(*args)


def heads_kernel(tokens, weights, out):
    def some_rows(k, carry):
        here = pl.ds(pl.multiple_of(k * 256, 256), 256)
        out[here, :] = lax.dot_general(
            tokens[here, :], weights[...], NT, preferred_element_type=F32
        ).astype(BF)
        return carry

    lax.fori_loop(0, 2, some_rows, 0)


def heads(*args):
    return pl.pallas_call(
        heads_kernel, out_shape=shape((512, 1536)), name="heads", compiler_params=room(12)
    )(*args)


def body(d_out, expert_ids, gate_weights, saved_gate, saved_up, w_gate, w_up, w_down, w_out):
    expert = lax.axis_index("expert").astype(I32)
    etp = lax.axis_index("etp").astype(I32)
    tp = lax.axis_index("tp").astype(I32)
    y, x = etp // 4, etp % 4
    core = tp % 2
    z = 4 * (tp // 2) + expert
    direction = 1 - 2 * core

    i = jnp.arange(34, dtype=I32)
    d, j, q = i // 4, i % 4, i % 8
    feature = 4 * ((y + jnp.where(core == 0, d, j)) % 4) + (x + jnp.where(core == 0, j, d)) % 4
    holder = jnp.where(i < 24, core, 1 - core)
    step = jnp.where(q >= 6, 4 * (q - 6), (1 - 2 * holder) * (q // 2 + 1))
    place = (z - step + 16) % 8
    source_core = jnp.where((q < 6) & (q % 2 == 1), 1 - holder, holder)
    table = jnp.where(i < 16, feature, 4 * (place % 4) + 2 * (place // 4) + source_core)
    table = jnp.where(i == 32, expert, jnp.where(i == 33, direction, table))

    near, far, sel = dispatch(table, expert_ids.T, gate_weights.T, d_out)
    other = swap_core(far)
    across = shift_z(near, 4)
    *sent, near = messages(far, other, near)
    received = []
    for k, rows in zip((1, 2, 3), sent):
        received.append(shift_z(rows, k))

    down_own, gate_own, up_own = w_down[0], w_gate[0], w_up[0]
    down_other = swap_core(down_own)
    gate_other = swap_core(gate_own)
    up_other = swap_core(up_own)
    factor_own, sent_factor = factors(table, saved_gate[0], saved_up[0])

    rows = pack(*received, near, across)
    ahead = shift_plane(rows, -1, True)
    behind = shift_plane(rows, 1, True)
    top, bottom = beside(rows, ahead, behind)
    top, bottom, sent_factor = lax.optimization_barrier((top, bottom, sent_factor))
    factor_other = swap_core(sent_factor)
    far_top = shift_plane(ahead[:256], -1, True)
    far_bottom = shift_plane(behind[256:], 1, True)
    far = jnp.concatenate([far_top, far_bottom], axis=0)

    behind_bottom = shift_plane(bottom, 1, False)
    ahead_top = shift_plane(top, -1, False)
    behind_far = shift_plane(far, 1, False)
    ahead_far = shift_plane(far, -1, False)
    behind_top = shift_plane(top, 1, False)
    ahead_bottom = shift_plane(bottom, -1, False)
    top_on, bottom_on = halves(ahead_top, ahead_far, behind_bottom, behind_far)
    last_top = shift_plane(top_on, -1, False)
    last_bottom = shift_plane(bottom_on, 1, False)

    acc = act_first(
        table,
        (top, bottom, far, ahead_top, ahead_bottom, ahead_far, behind_top, behind_bottom, behind_far),
        down_own,
        down_other,
    )
    grads = act_last(table, (last_top, last_bottom), down_own, down_other, acc, factor_own, factor_other)

    weights = (gate_own, gate_other, up_own, up_other)
    far_top, far_bottom = part(table, grads, weights, (2,), 2)
    got_top = shift_plane(far_top, 1, False)
    got_bottom = shift_plane(far_bottom, -1, False)
    ahead_top, ahead_bottom, ahead_far, behind_top, behind_bottom, behind_far = part(
        table, grads, weights, (1, 3), 2
    )
    from_behind_bottom = shift_plane(ahead_bottom, 1, False)
    from_ahead_top = shift_plane(behind_top, -1, False)
    own_near, own_far = part(table, grads, weights, (0,), 1)
    up_near, up_far, down_near, down_far = add_pairs(
        ahead_top, ahead_far, got_top, behind_bottom, behind_far, got_bottom
    )
    from_behind_far = shift_plane(up_far, 1, False)
    from_ahead_far = shift_plane(down_far, -1, False)
    from_behind_top = shift_plane(up_near, 1, False)
    from_ahead_bottom = shift_plane(down_near, -1, False)

    far_top, far_bottom = middle_far(own_far, from_behind_far, from_ahead_far)
    got_top = shift_plane(far_top, 1, True)
    got_bottom = shift_plane(far_bottom, -1, True)
    own, to_ahead, to_behind = middle_near(
        own_near,
        from_behind_top,
        from_ahead_top,
        from_behind_bottom,
        from_ahead_bottom,
        got_top,
        got_bottom,
    )
    from_behind = shift_plane(to_ahead, 1, True)
    from_ahead = shift_plane(to_behind, -1, True)
    *back, near, across = last(own, from_behind, from_ahead)

    across = shift_z(across, 4)
    returned = []
    for k, rows in zip((1, 2, 3), back):
        returned.append(shift_z(rows, -k))
    back = returned
    other = swap_core(jnp.concatenate([rows[64:128] for rows in back], axis=0))
    d_hidden = combine(sel, d_out, *back, other, near, across)

    head_partial = heads(lax.all_gather(d_hidden, "tp", axis=0, tiled=True), w_out)
    spread = lax.all_to_all(head_partial.reshape(16, 32, 1536), "etp", 0, 0, tiled=True)
    d_heads = jnp.sum(spread.astype(F32), axis=0).astype(BF)
    return (d_hidden, d_heads)


def solution(mesh):
    in_specs = (
        P(("expert", "tp"), "etp"),
        P(("expert", "tp"), None),
        P(("expert", "tp"), None),
        P("expert", None, ("etp", "tp")),
        P("expert", None, ("etp", "tp")),
        P("expert", None, ("etp", "tp")),
        P("expert", None, ("etp", "tp")),
        P("expert", ("etp", "tp"), None),
        P("tp", "etp"),
    )
    out_specs = (P(("expert", "tp"), "etp"), P(("expert", "etp"), "tp"))

    return jax.shard_map(body, mesh=mesh, in_specs=in_specs, out_specs=out_specs, check_vma=False)
```
